256 devices in a mesh: rows: 16 (over y, z_hi, core), feat: 16 (over z_lo, x).
Axes of the slice: x: 4, y: 4, z: 8 (z_hi: 2, z_lo: 4; z = z_hi * 4 + z_lo), core: 2. Of those that a mesh axis runs over, the one named last changes fastest.
Arguments:
- samples: float32 [24576, 8192], P('rows', 'feat'), may hold values from -6 to 6
- whitening: float32 [8192, 1024], P('feat', 'rows'), may hold values from -0.09375 to 0.09375
- components: float32 [1024, 1024], P('rows', 'feat'), may hold values from -0.25 to 0.25
Outputs:
- moment: float32 [1024, 1024], P('rows', 'feat')
The draws below stay inside these ranges and needn't reach their ends.
All inputs are finite; a program needn't handle non-finite values.
Results may differ from the reference program's by a relative error of at most 0.00017.
Values sent between devices are 32-bit elements; how exact they have to be, the bound alone decides.
A program may use at most 64 MiB of HBM per device.

```python
import jax
import jax.numpy as jnp
from jax import lax

F = 8192
K = 1024
R = 1024
ROWS = 24576


def strengthened(drawn, stream_key, source, target, blocks, factor):
    owner, partner = [(jnp.arange(drawn.shape[dim]) // (drawn.shape[dim] // blocks)).reshape([-1 if axis == dim else 1 for axis in range(drawn.ndim)]) for dim in (source, target)]
    chosen = jax.random.permutation(stream_key, blocks)[partner]
    strong = (owner == chosen) | (owner == (partner + blocks // 2) % blocks)
    return jnp.where(strong, factor * drawn, drawn)


def block_levels(own_key, shape, pieces, least, largest):
    def one(axis_at, blocks):
        heights = jax.random.uniform(jax.random.fold_in(jax.random.fold_in(own_key, 6), axis_at), (blocks,), jnp.float32, least / len(pieces), largest / len(pieces))
        return jnp.repeat(jnp.exp(heights), shape[axis_at] // blocks).reshape((-1,) + (1,) * (len(shape) - axis_at - 1))

    factor_of = one(*pieces[0])
    for cut in pieces[1:]:
        factor_of = factor_of * one(*cut)
    return factor_of


def bell_draw(key, extent, deviation, most, split=(), held_as=jnp.bfloat16):
    values = jax.random.normal(key, extent, jnp.float32) * deviation
    if len(split) > 0:
        values = block_levels(key, extent, split, -0.22, 0.18) * values
    return jnp.clip(values, min=-most, max=most).astype(held_as)


def heavy_noise(key, shape, deviation, limit, pieces, heavy, kind=jnp.bfloat16):
    array = deviation * jax.random.normal(key, shape, jnp.float32)
    if pieces:
        array = array * block_levels(key, shape, pieces, -0.22, 0.18)
    return jnp.clip(strengthened(array, jax.random.fold_in(key, 3), *heavy), -limit, limit).astype(kind)


def setup_inputs(seed: int = 0) -> dict:
    key_list = jax.random.split(jax.random.key(seed), 4)
    samples = bell_draw(key_list[0], (ROWS, F), 1.0, 6.0, ((0, 16), (1, 16)), jnp.float32)
    whitening = heavy_noise(key_list[1], (F, K), F ** -0.5, 0.09375, ((0, 16), (1, 16)), (0, 1, 16, 2.0), jnp.float32)
    components = heavy_noise(key_list[2], (K, R), K ** -0.5, 0.25, ((0, 16), (1, 16)), (0, 1, 16, 2.0), jnp.float32)
    return dict(samples=samples, whitening=whitening, components=components)


def reference(samples, whitening, components):
    whitened = jnp.dot(samples, whitening, precision=lax.Precision.HIGHEST, preferred_element_type=jnp.float32)
    projected = jnp.dot(whitened, components, precision=lax.Precision.HIGHEST, preferred_element_type=jnp.float32)
    squared = projected * projected
    total = lax.dot_general(whitened, squared, (((0,), (0,)), ((), ())), precision=lax.Precision.HIGHEST, preferred_element_type=jnp.float32)
    return total / jnp.sqrt(jnp.float32(ROWS))
```

```python
import jax
import jax.numpy as jnp
from jax import lax
from jax.experimental import pallas as pl
from jax.experimental.pallas import tpu as pltpu
from jax.sharding import PartitionSpec as P

MESH = pl.DeviceIdType.MESH
F32 = jnp.float32
BF16 = jnp.bfloat16
NX, NY, NZH, NZL, NC = 4, 4, 2, 4, 2
NZ = NZH * NZL
CH = NY * NZH
ROWS_DEV = 1536
BLK = ROWS_DEV // NX
HB = BLK // 2
SL = BLK // NZL
FD = 512


def split(v):
    hi = v.astype(BF16)
    return hi, (v - hi.astype(F32)).astype(BF16)


def nt(a, b):
    return lax.dot_general(a, b, (((1,), (1,)), ((), ())), preferred_element_type=F32)


def nn(a, b):
    return lax.dot_general(a, b, (((1,), (0,)), ((), ())), preferred_element_type=F32)


def three(dot, ah, al, bh, bl):
    return dot(ah, bh) + (dot(ah, bl) + dot(al, bh))


def kernel(
    s_hbm, w_hbm, c_hbm, out_hbm,
    sv, wv, cv, shi, slo, wall, whi, wlo,
    far, near, own, fr, nr, zb, zr, av, ahi, alo,
    ctp, cx, ct, chi, clo, pt, qhi, qlo, mb, mp, ms, mr, fs, frec, gv, gr, ov, ot, of,
    lsem, wsend, wrecv, wpsend, wprecv, xsend, xrecv, zsend, zrecv, ysend, yrecv,
    csend, crecv, rsend, rrecv, psend, precv, msend, mrecv, fsend, frecv,
):
    i, j = lax.axis_index("rows"), lax.axis_index("feat")
    y, zh, c = i // 4, (i // 2) % 2, i % 2
    zl, x = j // 4, j % 4
    z = zh * 4 + zl
    xl, xr = (x + 3) % 4, (x + 1) % 4

    def dev(y_=None, zh_=None, c_=None, zl_=None, x_=None):
        y_ = y if y_ is None else y_
        zh_ = zh if zh_ is None else zh_
        c_ = c if c_ is None else c_
        zl_ = zl if zl_ is None else zl_
        x_ = x if x_ is None else x_
        return (y_ * 4 + zh_ * 2 + c_, zl_ * 4 + x_)

    def devz(z_, **kw):
        return dev(zh_=z_ // 4, zl_=z_ % 4, **kw)

    def rc(src, dst, ss, rs, to):
        return pltpu.make_async_remote_copy(
            src_ref=src, dst_ref=dst, send_sem=ss, recv_sem=rs, device_id=to, device_id_type=MESH
        )

    def chunk(y_, t):
        u = t % 4
        dy = u + (u // 2) * (1 - 2 * (u % 2))
        return ((y_ + dy) % 4) * 2 + (zh + t // 4) % 2

    wcopy = pltpu.make_async_copy(w_hbm, wv, lsem.at[0])
    ccopy = pltpu.make_async_copy(c_hbm, cv, lsem.at[1])
    wcopy.start()

    def scopy(d):
        rows = pl.ds(pl.multiple_of(((x + d) % 4) * BLK, BLK), BLK)
        return pltpu.make_async_copy(s_hbm.at[rows], sv.at[rows], lsem.at[2 + d])

    for d in (2, 1, 3, 0):
        scopy(d).start()
    ccopy.start()

    barrier = pltpu.get_barrier_semaphore()
    partners = [dev(x_=(x + d) % 4) for d in (1, 2, 3)]
    partners += [dev(y_=(y + d) % 4) for d in (1, 2, 3)]
    partners += [dev(zl_=(zl + d) % 4) for d in (1, 2, 3)]
    partners += [dev(zh_=1 - zh), dev(c_=1 - c), devz((z + 1) % 8), devz((z + 7) % 8)]
    partners += [dev(y_=zl, zl_=y, x_=d) for d in range(4)]
    partners += [devz(d, y_=zl) for d in range(8)]
    for p in partners:
        pl.semaphore_signal(barrier, inc=1, device_id=p, device_id_type=MESH)

    wcopy.wait()
    wt = wv[...].T
    q0 = chunk(y, 0)
    wall[q0, c] = wt

    pl.semaphore_wait(barrier, len(partners))

    def wy(base, q, d, t):
        return rc(wall.at[q, c], wall.at[q, c], wsend.at[base + d], wrecv.at[t], dev(y_=(y + d) % 4))

    def wz():
        return rc(wall.at[q0, c], wall.at[q0, c], wsend.at[4], wrecv.at[4], dev(zh_=1 - zh))

    def wp(t):
        q = chunk(y, t)
        return rc(wall.at[q, c], wall.at[q, c], wpsend.at[t], wprecv.at[t], dev(c_=1 - c))

    def w_arrived(t):
        q = chunk(y, t)
        rc(wall.at[q, c], wall.at[q, c], wsend.at[0], wrecv.at[t], dev(c_=1 - c)).wait_recv()

    def wp_arrived(t):
        q = chunk(y, t)
        rc(wall.at[q, c], wall.at[q, 1 - c], wpsend.at[t], wprecv.at[t], dev(c_=1 - c)).wait_recv()

    wp(0).start()
    wy(0, q0, 3, 1).start()
    wy(0, q0, 1, 2).start()
    wy(0, q0, 2, 3).start()
    wz().start()

    def split_s(d):
        scopy(d).wait()

        def body(n, _):
            rows = pl.ds(pl.multiple_of(((x + d) % 4) * BLK + n * 96, 96), 96)
            h, l = split(sv[rows, :])
            shi[rows, :] = h
            slo[rows, :] = l
            return 0

        lax.fori_loop(0, BLK // 96, body, 0)

    split_s(2)

    ccopy.wait()
    ct_own = cv[...].T
    cz = jnp.zeros((64, 64), F32)
    at0 = jnp.concatenate([ct_own, cz], axis=1)
    at1 = jnp.concatenate([cz, ct_own], axis=1)
    ctp[...] = jnp.where(c == 0, at0, at1).reshape(2, 32, 128)

    def c_swap():
        return rc(ctp.at[1 - c], cx, csend.at[0], crecv.at[0], dev(c_=1 - c))

    c_swap().start()
    qc = zl * 2 + zh

    def c_out(d):
        return rc(ctp.at[c], ct.at[c, y * 2 + zh, x], csend.at[1 + d], crecv.at[1 + x], dev(y_=zl, zl_=y, x_=d))

    def c_keep():
        return pltpu.make_async_copy(ctp.at[c], ct.at[c, y * 2 + zh, x], lsem.at[6])

    def c_in(d):
        return rc(ctp.at[c], ct.at[c, qc, d], csend.at[1 + d], crecv.at[1 + d], dev(y_=zl, zl_=y, x_=d))

    diagonal = y == zl

    def unit(z_):
        return ((z_ % 4) * 2 + z_ // 4) % 8

    def ring_r(k):
        q = unit((z + 9 - k) % 8)
        return rc(ct.at[c, q], ct.at[c, q], rsend.at[0, k], rrecv.at[0, k], devz((z + 1) % 8))

    def ring_l(k):
        q = unit((z + k + 7) % 8)
        return rc(ct.at[c, q], ct.at[c, q], rsend.at[1, k], rrecv.at[1, k], devz((z + 7) % 8))

    def ring_r_in(k):
        q = unit((z + 8 - k) % 8)
        return rc(ct.at[c, q], ct.at[c, q], rsend.at[0, k], rrecv.at[0, k], devz((z + 7) % 8))

    def ring_l_in(k):
        q = unit((z + k) % 8)
        return rc(ct.at[c, q], ct.at[c, q], rsend.at[1, k], rrecv.at[1, k], devz((z + 1) % 8))

    def c_pair():
        return rc(ct.at[c], ct.at[c], psend.at[0], precv.at[0], dev(c_=1 - c))

    def c_pair_in():
        return rc(ct.at[1 - c], ct.at[1 - c], psend.at[0], precv.at[0], dev(c_=1 - c))

    def block(t, d, half):
        rows = pl.ds(pl.multiple_of(((x + d) % 4) * BLK + half * HB, HB), HB)
        return three(nt, shi[rows, :], slo[rows, :], whi[t], wlo[t])

    def x_copy(t, m):
        src, dst, to = (
            (far.at[t, 0], fr.at[t, 0], xr),
            (far.at[t, 1], fr.at[t, 1], xl),
            (near.at[t, 0, 1], nr.at[t, 0, 1], xr),
            (near.at[t, 1, 0], nr.at[t, 1, 0], xl),
            (near.at[t, 0, 0], nr.at[t, 0, 0], xr),
            (near.at[t, 1, 1], nr.at[t, 1, 1], xl),
        )[m]
        return rc(src, dst, xsend.at[t, m], xrecv.at[t, m], dev(x_=to))

    def z_copy(t, d):
        return rc(zb.at[t, (zl + d) % 4], zr.at[t, d - 1], zsend.at[t, d - 1], zrecv.at[t, d - 1], dev(zl_=(zl + d) % 4))

    def y_copy(t, d):
        q = chunk(y, t)
        return rc(av.at[q, y], av.at[q, y], ysend.at[t, d - 1], yrecv.at[t, d - 1], dev(y_=(y + d) % 4))

    def y_in(t, d):
        yo = (y + 4 - d) % 4
        q = chunk(yo, t)
        return rc(av.at[q, yo], av.at[q, yo], ysend.at[t, d - 1], yrecv.at[t, d - 1], dev(y_=yo))

    def far_step(t):
        q = chunk(y, t)
        h, l = split(wall[q].reshape(128, FD))
        whi[t] = h
        wlo[t] = l
        for half in range(2):
            far[t, half] = block(t, 2, half)
            x_copy(t, half).start()

    def near_step(t):
        near[t, 0, 1] = block(t, 1, 1)
        x_copy(t, 2).start()
        near[t, 1, 0] = block(t, 3, 0)
        x_copy(t, 3).start()
        near[t, 0, 0] = block(t, 1, 0)
        near[t, 1, 1] = block(t, 3, 1)

    def join_step(t):
        for side in range(2):
            x_copy(t, side).wait_recv()
            near[t, side, side] = near[t, side, side] + fr[t, side]
            x_copy(t, 4 + side).start()

    def own_step(t):
        for half in range(2):
            own[t, half] = block(t, 0, half)

    def x_finish(t):
        for m in range(2, 6):
            x_copy(t, m).wait_recv()
        for half in range(2):
            v = own[t, half] + nr[t, 0, half] + nr[t, 1, half]
            zb[t, 2 * half] = v[:SL]
            zb[t, 2 * half + 1] = v[SL:]
        for d in (2, 1, 3):
            z_copy(t, d).start()

    def keep(q, yo):
        h, l = split(av[q, yo])
        rows = pl.ds(pl.multiple_of(yo * SL, SL), SL)
        cols = pl.ds(pl.multiple_of(q * 128, 128), 128)
        ahi[rows, cols] = h
        alo[rows, cols] = l

    def z_finish(t):
        for d in (1, 2, 3):
            z_copy(t, d).wait_recv()
        q = chunk(y, t)
        av[q, y] = (zb[t, zl] + zr[t, 0]) + (zr[t, 1] + zr[t, 2])
        for d in (2, 1, 3):
            y_copy(t, d).start()
        keep(q, y)

    def y_finish(t):
        for d in (1, 2, 3):
            y_in(t, d).wait_recv()
            yo = (y + 4 - d) % 4
            keep(chunk(yo, t), yo)

    wp_arrived(0)
    far_step(0)
    for d in (1, 3, 0):
        split_s(d)

    def step(t, _):
        near_step(t)

        @pl.when((t < 7) & (t != 3))
        def _():
            w_arrived(t + 1)
            wp(t + 1).start()

        @pl.when(t == 2)
        def _():
            w_arrived(4)
            q = chunk(y, 4)
            wp(4).start()
            wy(4, q, 3, 5).start()
            wy(4, q, 1, 6).start()
            wy(4, q, 2, 7).start()

        join_step(t)

        @pl.when(t < 7)
        def _():
            wp_arrived(t + 1)
            far_step(t + 1)

        @pl.when(t == 0)
        def _():
            c_swap().wait()
            ctp[c] = ctp[c] + cx[...]
            for d in range(4):

                @pl.when(jnp.logical_not(diagonal & (x == d)))
                def _(d=d):
                    c_out(d).start()

            @pl.when(diagonal)
            def _():
                c_keep().start()
                c_keep().wait()

        @pl.when(t == 1)
        def _():
            for d in range(4):

                @pl.when(jnp.logical_not(diagonal & (x == d)))
                def _(d=d):
                    c_in(d).wait_recv()
                    c_out(d).wait_send()

            ring_r(1).start()
            ring_l(1).start()

        @pl.when((t >= 2) & (t < 6))
        def _():
            ring_r_in(t - 1).wait_recv()
            ring_r(t - 1).wait_send()

        @pl.when((t >= 2) & (t < 5))
        def _():
            ring_r(t).start()
            ring_l_in(t - 1).wait_recv()
            ring_l(t - 1).wait_send()

        @pl.when((t >= 2) & (t < 4))
        def _():
            ring_l(t).start()

        @pl.when(t == 5)
        def _():
            c_pair().start()

        own_step(t)

        @pl.when(t >= 1)
        def _():
            x_finish(t - 1)

        @pl.when(t >= 2)
        def _():
            z_finish(t - 2)

        @pl.when(t >= 3)
        def _():
            y_finish(t - 3)

        return 0

    lax.fori_loop(0, CH, step, 0)
    x_finish(7)
    z_finish(6)
    y_finish(5)

    c_pair().wait_send()
    c_pair_in().wait_recv()

    def split_c(n, _):
        half, q = n // 8, n % 8
        h, l = split(ct[half, q].reshape(128, 128))
        cols = pl.ds(pl.multiple_of(q * 128, 128), 128)
        chi[half, :, cols] = h
        clo[half, :, cols] = l
        return 0

    lax.fori_loop(0, 16, split_c, 0)

    z_finish(7)
    y_finish(6)
    y_finish(7)

    for half in range(2):
        v = three(nt, chi[half], clo[half], ahi[...], alo[...])
        h, l = split(v * v)
        qhi[half] = h
        qlo[half] = l

    def moment_half(half):
        qh, ql = qhi[half], qlo[half]

        def body(n, _):
            cols = pl.ds(pl.multiple_of(n * 256, 256), 256)
            v = three(nn, qh, ql, ahi[:, cols], alo[:, cols])
            for u in range(2):
                mb[half, :, 2 * n + u] = v[:, 128 * u : 128 * u + 128].reshape(4, 32, 128)
            return 0

        lax.fori_loop(0, 4, body, 0)

    def m_pair():
        return rc(mb.at[1 - c], mp, psend.at[1], precv.at[1], dev(c_=1 - c))

    moment_half(1 - c)
    m_pair().start()
    moment_half(c)
    m_pair().wait_recv()

    def m_copy(d):
        return rc(ms.at[(x + d) % 4], mr.at[d - 1], msend.at[d], mrecv.at[d], dev(x_=(x + d) % 4))

    for d in (2, 1, 3, 0):
        b = (x + d) % 4
        ms[b] = mb[c, b] + mp[b]
        if d:
            m_copy(d).start()
    for d in (1, 2, 3):
        m_copy(d).wait_recv()
    fs[...] = (ms[x] + mr[0]) + (mr[1] + mr[2])

    def f_out(q):
        return rc(fs.at[q], frec.at[z], fsend.at[q], frecv.at[z], dev(y_=q // 2, zh_=q % 2, zl_=y))

    def f_in(z_):
        return rc(fs.at[0], frec.at[z_], fsend.at[0], frecv.at[z_], devz(z_, y_=zl))

    mine = y * 2 + zh
    for q in range(8):

        @pl.when(jnp.logical_not(diagonal & (q == mine)))
        def _(q=q):
            f_out(q).start()

    @pl.when(diagonal)
    def _():
        frec[z] = fs[mine]

    for z_ in range(8):

        @pl.when(jnp.logical_not(diagonal & (z == z_)))
        def _(z_=z_):
            f_in(z_).wait_recv()

    total = frec[0]
    for z_ in range(1, 8):
        total = total + frec[z_]
    gv[...] = total * (1.0 / 24576.0**0.5)
    swap = rc(gv, gr, psend.at[2], precv.at[2], dev(c_=1 - c))
    swap.start()
    ov[pl.ds(pl.multiple_of(c * 32, 32), 32), :] = gv[...]
    swap.wait_recv()
    ov[pl.ds(pl.multiple_of((1 - c) * 32, 32), 32), :] = gr[...]
    ot[...] = ov[...].T
    of[...] = ot[pl.ds(pl.multiple_of(c * 64, 64), 64), :]
    result = pltpu.make_async_copy(of, out_hbm, lsem.at[7])
    result.start()

    swap.wait_send()
    m_pair().wait_send()
    for d in (1, 2, 3):
        m_copy(d).wait_send()
        wy(0, q0, d, d).wait_send()
        wy(4, chunk(y, 4), d, d).wait_send()
    wz().wait_send()
    for q in range(8):

        @pl.when(jnp.logical_not(diagonal & (q == mine)))
        def _(q=q):
            f_out(q).wait_send()

    def drain(t, _):
        wp(t).wait_send()
        for m in range(6):
            x_copy(t, m).wait_send()
        for d in (1, 2, 3):
            z_copy(t, d).wait_send()
            y_copy(t, d).wait_send()
        return 0

    lax.fori_loop(0, CH, drain, 0)
    result.wait()


def on_device(samples, whitening, components):
    V = pltpu.VMEM
    D = pltpu.SemaphoreType.DMA
    scratch = [
        V((ROWS_DEV, FD), F32), V((FD, 64), F32), V((64, 64), F32),
        V((ROWS_DEV, FD), BF16), V((ROWS_DEV, FD), BF16),
        V((CH, NC, 64, FD), F32), V((CH, 128, FD), BF16), V((CH, 128, FD), BF16),
        V((CH, 2, HB, 128), F32), V((CH, 2, 2, HB, 128), F32), V((CH, 2, HB, 128), F32),
        V((CH, 2, HB, 128), F32), V((CH, 2, 2, HB, 128), F32),
        V((CH, 4, SL, 128), F32), V((CH, 3, SL, 128), F32),
        V((CH, NY, SL, 128), F32), V((BLK, 1024), BF16), V((BLK, 1024), BF16),
        V((2, 32, 128), F32), V((32, 128), F32), V((2, 8, 4, 32, 128), F32),
        V((2, 128, 1024), BF16), V((2, 128, 1024), BF16),
        V((8, 128), F32), V((2, 128, BLK), BF16), V((2, 128, BLK), BF16),
        V((2, 4, 8, 32, 128), F32), V((4, 8, 32, 128), F32), V((4, 8, 32, 128), F32),
        V((3, 8, 32, 128), F32), V((8, 32, 128), F32), V((8, 32, 128), F32),
        V((32, 128), F32), V((32, 128), F32), V((64, 128), F32), V((128, 64), F32), V((64, 64), F32),
        D((8,)), D((8,)), D((8,)), D((8,)), D((8,)),
        D((8, 6)), D((8, 6)), D((8, 3)), D((8, 3)), D((8, 3)), D((8, 3)),
        D((5,)), D((5,)), D((2, 5)), D((2, 5)), D((3,)), D((3,)), D((4,)), D((4,)), D((8,)), D((8,)),
    ]
    return pl.pallas_call(
        kernel,
        out_shape=jax.ShapeDtypeStruct((64, 64), F32),
        in_specs=[pl.BlockSpec(memory_space=pl.ANY)] * 3,
        out_specs=pl.BlockSpec(memory_space=pl.ANY),
        scratch_shapes=scratch,
        compiler_params=pltpu.CompilerParams(
            collective_id=0, has_side_effects=True, vmem_limit_bytes=60 * 1024 * 1024
        ),
    )(samples, whitening, components)


def solution(mesh):
    placed = (P("rows", "feat"), P("feat", "rows"), P("rows", "feat"))
    return jax.shard_map(
        on_device, mesh=mesh, in_specs=placed, out_specs=P("rows", "feat"), check_vma=False
    )
```

```python
import jax
import jax.numpy as jnp
from jax import lax
from jax.experimental import pallas as pl
from jax.experimental.pallas import tpu as pltpu
from jax.sharding import PartitionSpec as P

MESH = pl.DeviceIdType.MESH
F32 = jnp.float32
BF16 = jnp.bfloat16
NX, NY, NZH, NZL, NC = 4, 4, 2, 4, 2
NZ = NZH * NZL
CH = NY * NZH
ROWS_DEV = 1536
BLK = ROWS_DEV // NX
HB = BLK // 2
SL = BLK // NZL
FD = 512


def split(v):
    hi = v.astype(BF16)
    return hi, (v - hi.astype(F32)).astype(BF16)


def nt(a, b):
    return lax.dot_general(a, b, (((1,), (1,)), ((), ())), preferred_element_type=F32)


def nn(a, b):
    return lax.dot_general(a, b, (((1,), (0,)), ((), ())), preferred_element_type=F32)


def three(dot, ah, al, bh, bl):
    return dot(ah, bh) + (dot(ah, bl) + dot(al, bh))


def kernel(
    s_hbm, w_hbm, c_hbm, out_hbm,
    sv, cv, shi, slo, wall, whi, wlo,
    far, near, own, fr, nr, zb, zr, av, ahi, alo,
    ctp, cx, ct, chi, clo, pt, qhi, qlo, mb, mp, ms, mf, mr, fs, frec, gv, gr, ov, ot, of,
    lsem, wsend, wrecv, wpsend, wprecv, xsend, xrecv, zsend, zrecv, ysend, yrecv,
    csend, crecv, rsend, rrecv, psend, precv, msend, mrecv, fsend, frecv,
):
    i, j = lax.axis_index("rows"), lax.axis_index("feat")
    y, zh, c = i // 4, (i // 2) % 2, i % 2
    zl, x = j // 4, j % 4
    z = zh * 4 + zl
    xl, xr = (x + 3) % 4, (x + 1) % 4

    def dev(y_=None, zh_=None, c_=None, zl_=None, x_=None):
        y_ = y if y_ is None else y_
        zh_ = zh if zh_ is None else zh_
        c_ = c if c_ is None else c_
        zl_ = zl if zl_ is None else zl_
        x_ = x if x_ is None else x_
        return (y_ * 4 + zh_ * 2 + c_, zl_ * 4 + x_)

    def devz(z_, **kw):
        return dev(zh_=z_ // 4, zl_=z_ % 4, **kw)

    def rc(src, dst, ss, rs, to):
        return pltpu.make_async_remote_copy(
            src_ref=src, dst_ref=dst, send_sem=ss, recv_sem=rs, device_id=to, device_id_type=MESH
        )

    def chunk(y_, t):
        u = t % 4
        dy = u + (u // 2) * (1 - 2 * (u % 2))
        return ((y_ + dy) % 4) * 2 + (zh + t // 4) % 2

    q0 = chunk(y, 0)
    wcopy = pltpu.make_async_copy(w_hbm, wall.at[q0, c], lsem.at[0])
    ccopy = pltpu.make_async_copy(c_hbm, cv, lsem.at[1])
    wcopy.start()

    def scopy(d):
        rows = pl.ds(pl.multiple_of(((x + d) % 4) * BLK, BLK), BLK)
        return pltpu.make_async_copy(s_hbm.at[rows], sv.at[rows], lsem.at[2 + d])

    for d in (2, 1, 3, 0):
        scopy(d).start()
    ccopy.start()

    barrier = pltpu.get_barrier_semaphore()
    partners = [dev(x_=(x + d) % 4) for d in (1, 2, 3)]
    partners += [dev(y_=(y + d) % 4) for d in (1, 2, 3)]
    partners += [dev(zl_=(zl + d) % 4) for d in (1, 2, 3)]
    partners += [dev(zh_=1 - zh), dev(c_=1 - c), devz((z + 1) % 8), devz((z + 7) % 8)]
    partners += [dev(y_=zl, zl_=y, x_=d) for d in range(4)]
    partners += [devz(d, y_=zl) for d in range(8)]
    for p in partners:
        pl.semaphore_signal(barrier, inc=1, device_id=p, device_id_type=MESH)

    wcopy.wait()
    pl.semaphore_wait(barrier, len(partners))

    def wy(base, q, d, t):
        return rc(wall.at[q, c], wall.at[q, c], wsend.at[base + d], wrecv.at[t], dev(y_=(y + d) % 4))

    def wz():
        return rc(wall.at[q0, c], wall.at[q0, c], wsend.at[4], wrecv.at[4], dev(zh_=1 - zh))

    def wp(t):
        q = chunk(y, t)
        return rc(wall.at[q, c], wall.at[q, c], wpsend.at[t], wprecv.at[t], dev(c_=1 - c))

    def w_arrived(t):
        q = chunk(y, t)
        rc(wall.at[q, c], wall.at[q, c], wsend.at[0], wrecv.at[t], dev(c_=1 - c)).wait_recv()

    def wp_arrived(t):
        q = chunk(y, t)
        rc(wall.at[q, c], wall.at[q, 1 - c], wpsend.at[t], wprecv.at[t], dev(c_=1 - c)).wait_recv()

    wp(0).start()
    wy(0, q0, 3, 1).start()
    wy(0, q0, 1, 2).start()
    wy(0, q0, 2, 3).start()
    wz().start()

    def split_s(d):
        scopy(d).wait()

        def body(n, _):
            rows = pl.ds(pl.multiple_of(((x + d) % 4) * BLK + n * 96, 96), 96)
            h, l = split(sv[rows, :])
            shi[rows, :] = h
            slo[rows, :] = l
            return 0

        lax.fori_loop(0, BLK // 96, body, 0)

    split_s(2)

    ccopy.wait()
    ct_own = cv[...].T
    cz = jnp.zeros((64, 64), F32)
    at0 = jnp.concatenate([ct_own, cz], axis=1)
    at1 = jnp.concatenate([cz, ct_own], axis=1)
    ctp[...] = jnp.where(c == 0, at0, at1).reshape(2, 32, 128)

    def c_swap():
        return rc(ctp.at[1 - c], cx, csend.at[0], crecv.at[0], dev(c_=1 - c))

    c_swap().start()
    qc = zl * 2 + zh

    def c_out(d):
        return rc(ctp.at[c], ct.at[c, y * 2 + zh, x], csend.at[1 + d], crecv.at[1 + x], dev(y_=zl, zl_=y, x_=d))

    def c_keep():
        return pltpu.make_async_copy(ctp.at[c], ct.at[c, y * 2 + zh, x], lsem.at[6])

    def c_in(d):
        return rc(ctp.at[c], ct.at[c, qc, d], csend.at[1 + d], crecv.at[1 + d], dev(y_=zl, zl_=y, x_=d))

    diagonal = y == zl

    def unit(z_):
        return ((z_ % 4) * 2 + z_ // 4) % 8

    def ring_r(k):
        q = unit((z + 9 - k) % 8)
        return rc(ct.at[c, q], ct.at[c, q], rsend.at[0, k], rrecv.at[0, k], devz((z + 1) % 8))

    def ring_l(k):
        q = unit((z + k + 7) % 8)
        return rc(ct.at[c, q], ct.at[c, q], rsend.at[1, k], rrecv.at[1, k], devz((z + 7) % 8))

    def ring_r_in(k):
        q = unit((z + 8 - k) % 8)
        return rc(ct.at[c, q], ct.at[c, q], rsend.at[0, k], rrecv.at[0, k], devz((z + 7) % 8))

    def ring_l_in(k):
        q = unit((z + k) % 8)
        return rc(ct.at[c, q], ct.at[c, q], rsend.at[1, k], rrecv.at[1, k], devz((z + 1) % 8))

    def c_pair():
        return rc(ct.at[c], ct.at[c], psend.at[0], precv.at[0], dev(c_=1 - c))

    def c_pair_in():
        return rc(ct.at[1 - c], ct.at[1 - c], psend.at[0], precv.at[0], dev(c_=1 - c))

    def block(t, d):
        rows = pl.ds(pl.multiple_of(((x + d) % 4) * BLK, BLK), BLK)
        return three(nt, shi[rows, :], slo[rows, :], whi[t], wlo[t])

    def x_copy(t, m):
        src, dst, to = (
            (far.at[t, 0], fr.at[t, 0], xr),
            (far.at[t, 1], fr.at[t, 1], xl),
            (near.at[t, 0, 1], nr.at[t, 0, 1], xr),
            (near.at[t, 1, 0], nr.at[t, 1, 0], xl),
            (near.at[t, 0, 0], nr.at[t, 0, 0], xr),
            (near.at[t, 1, 1], nr.at[t, 1, 1], xl),
        )[m]
        return rc(src, dst, xsend.at[t, m], xrecv.at[t, m], dev(x_=to))

    def z_copy(t, d):
        return rc(zb.at[t, (zl + d) % 4], zr.at[t, d - 1], zsend.at[t, d - 1], zrecv.at[t, d - 1], dev(zl_=(zl + d) % 4))

    def y_copy(t, d):
        q = chunk(y, t)
        return rc(av.at[q, y], av.at[q, y], ysend.at[t, d - 1], yrecv.at[t, d - 1], dev(y_=(y + d) % 4))

    def y_in(t, d):
        yo = (y + 4 - d) % 4
        q = chunk(yo, t)
        return rc(av.at[q, yo], av.at[q, yo], ysend.at[t, d - 1], yrecv.at[t, d - 1], dev(y_=yo))

    def far_step(t):
        q = chunk(y, t)

        def body(n, _):
            h, l = split(wall[q, n])
            rows = pl.ds(pl.multiple_of(n * 64, 64), 64)
            whi[t, rows, :] = h
            wlo[t, rows, :] = l
            return 0

        lax.fori_loop(0, NC, body, 0)
        far[t] = block(t, 2).reshape(2, HB, 128)
        x_copy(t, 0).start()
        x_copy(t, 1).start()

    def near_step(t):
        near[t, 0] = block(t, 1).reshape(2, HB, 128)
        x_copy(t, 2).start()
        near[t, 1] = block(t, 3).reshape(2, HB, 128)
        x_copy(t, 3).start()

    def join_step(t):
        for side in range(2):
            x_copy(t, side).wait_recv()
            near[t, side, side] = near[t, side, side] + fr[t, side]
            x_copy(t, 4 + side).start()

    def own_step(t):
        own[t] = block(t, 0).reshape(2, HB, 128)

    def x_finish(t):
        for m in range(2, 6):
            x_copy(t, m).wait_recv()
        for half in range(2):
            v = own[t, half] + nr[t, 0, half] + nr[t, 1, half]
            zb[t, 2 * half] = v[:SL]
            zb[t, 2 * half + 1] = v[SL:]
        for d in (2, 1, 3):
            z_copy(t, d).start()

    def keep(q, yo):
        h, l = split(av[q, yo])
        rows = pl.ds(pl.multiple_of(yo * 128, 128), SL)
        cols = pl.ds(pl.multiple_of(q * 128, 128), 128)
        ahi[rows, cols] = h
        alo[rows, cols] = l

    def z_finish(t):
        for d in (1, 2, 3):
            z_copy(t, d).wait_recv()
        q = chunk(y, t)
        av[q, y] = (zb[t, zl] + zr[t, 0]) + (zr[t, 1] + zr[t, 2])
        for d in (2, 1, 3):
            y_copy(t, d).start()
        keep(q, y)

    def y_finish(t):
        for d in (1, 2, 3):
            y_in(t, d).wait_recv()
            yo = (y + 4 - d) % 4
            keep(chunk(yo, t), yo)

    for slot in range(NY):
        ahi[128 * slot + SL : 128 * slot + 128, :] = jnp.zeros((128 - SL, 1024), BF16)
        alo[128 * slot + SL : 128 * slot + 128, :] = jnp.zeros((128 - SL, 1024), BF16)
    wp_arrived(0)
    far_step(0)
    for d in (1, 3, 0):
        split_s(d)

    def step(t, _):
        near_step(t)

        @pl.when(t == 0)
        def _():
            w_arrived(1)
            wp(1).start()

        @pl.when(t < 6)
        def _():
            w_arrived(t + 2)
            wp(t + 2).start()

        @pl.when(t == 2)
        def _():
            q = chunk(y, 4)
            wy(4, q, 3, 5).start()
            wy(4, q, 1, 6).start()
            wy(4, q, 2, 7).start()

        join_step(t)

        @pl.when(t < 7)
        def _():
            wp_arrived(t + 1)
            far_step(t + 1)

        @pl.when(t == 0)
        def _():
            c_swap().wait()
            ctp[c] = ctp[c] + cx[...]
            for d in range(4):

                @pl.when(jnp.logical_not(diagonal & (x == d)))
                def _(d=d):
                    c_out(d).start()

            @pl.when(diagonal)
            def _():
                c_keep().start()
                c_keep().wait()

        @pl.when(t == 2)
        def _():
            for d in range(4):

                @pl.when(jnp.logical_not(diagonal & (x == d)))
                def _(d=d):
                    c_in(d).wait_recv()
                    c_out(d).wait_send()

            ring_r(1).start()
            ring_l(1).start()

        @pl.when((t >= 3) & (t < 7))
        def _():
            ring_r_in(t - 2).wait_recv()
            ring_r(t - 2).wait_send()

        @pl.when((t >= 3) & (t < 6))
        def _():
            ring_r(t - 1).start()
            ring_l_in(t - 2).wait_recv()
            ring_l(t - 2).wait_send()

        @pl.when((t >= 3) & (t < 5))
        def _():
            ring_l(t - 1).start()

        @pl.when(t == 6)
        def _():
            c_pair().start()

        own_step(t)

        @pl.when(t >= 1)
        def _():
            x_finish(t - 1)

        @pl.when(t >= 3)
        def _():
            z_finish(t - 3)

        @pl.when(t >= 5)
        def _():
            y_finish(t - 5)

        return 0

    lax.fori_loop(0, CH, step, 0)
    z_finish(5)
    x_finish(7)
    y_finish(3)
    z_finish(6)
    y_finish(4)

    c_pair().wait_send()
    c_pair_in().wait_recv()

    def split_c(q, _):
        cols = pl.ds(pl.multiple_of(q * 128, 128), 128)
        for half in range(2):
            h, l = split(ct[half, q].reshape(128, 128))
            chi[128 * half : 128 * half + 128, cols] = h
            clo[128 * half : 128 * half + 128, cols] = l
        return 0

    lax.fori_loop(0, 8, split_c, 0)
    y_finish(5)

    def project(t, d):
        yo = (y + 4 - d) % 4
        cols = pl.ds(pl.multiple_of(chunk(yo, t) * 128, 128), 128)
        slot = pl.ds(pl.multiple_of(yo * 128, 128), 128)
        pt[:, slot] = pt[:, slot] + three(nt, chi[:, cols], clo[:, cols], ahi[slot, cols], alo[slot, cols])

    def project_some(n, _):
        project(n // 4, n % 4)
        return 0

    pt[...] = jnp.zeros_like(pt)
    lax.fori_loop(0, 24, project_some, 0)
    z_finish(7)
    y_finish(6)
    lax.fori_loop(24, 29, project_some, 0)
    y_finish(7)
    lax.fori_loop(29, 32, project_some, 0)

    h, l = split(pt[...] * pt[...])
    qhi[...] = h.reshape(2, 128, 512)
    qlo[...] = l.reshape(2, 128, 512)

    def moment_part(half, part):
        def body(n, _):
            cols = pl.ds(pl.multiple_of(part * 512 + n * 256, 256), 256)
            v = three(nn, qhi[half], qlo[half], ahi[:, cols], alo[:, cols])
            for u in range(2):
                mb[half, part, :, 2 * n + u] = v[:, 128 * u : 128 * u + 128].reshape(4, 32, 128)
            return 0

        lax.fori_loop(0, 2, body, 0)

    def m_pair(part):
        return rc(mb.at[1 - c, part], mp.at[part], psend.at[1 + part], precv.at[1 + part], dev(c_=1 - c))

    for part in range(2):
        moment_part(1 - c, part)
        m_pair(part).start()
    for part in range(2):
        moment_part(c, part)

    def m_copy(m):
        src, dst, to = (
            (ms.at[(x + 2) % 4, 0], mf.at[0], xr),
            (ms.at[(x + 2) % 4, 1], mf.at[1], xl),
            (ms.at[xr, 1], mr.at[0, 1], xr),
            (ms.at[xl, 0], mr.at[1, 0], xl),
            (ms.at[xr, 0], mr.at[0, 0], xr),
            (ms.at[xl, 1], mr.at[1, 1], xl),
        )[m]
        return rc(src, dst, msend.at[m], mrecv.at[m], dev(x_=to))

    def m_sum(b, part):
        ms[b, part] = mb[c, part, b] + mp[part, b]

    m_pair(0).wait_recv()
    m_sum((x + 2) % 4, 0)
    m_copy(0).start()
    m_sum(xl, 0)
    m_copy(3).start()
    m_pair(1).wait_recv()
    m_sum((x + 2) % 4, 1)
    m_copy(1).start()
    m_sum(xr, 1)
    m_copy(2).start()
    m_sum(xr, 0)
    m_copy(0).wait_recv()
    ms[xr, 0] = ms[xr, 0] + mf[0]
    m_copy(4).start()
    m_sum(xl, 1)
    m_copy(1).wait_recv()
    ms[xl, 1] = ms[xl, 1] + mf[1]
    m_copy(5).start()
    m_sum(x, 0)
    m_sum(x, 1)
    for m in range(2, 6):
        m_copy(m).wait_recv()
    fs[...] = ms[x].reshape(8, 32, 128) + (mr[0] + mr[1]).reshape(8, 32, 128)

    def f_out(q):
        return rc(fs.at[q], frec.at[z], fsend.at[q], frecv.at[z], dev(y_=q // 2, zh_=q % 2, zl_=y))

    def f_in(z_):
        return rc(fs.at[0], frec.at[z_], fsend.at[0], frecv.at[z_], devz(z_, y_=zl))

    mine = y * 2 + zh
    for q in range(8):

        @pl.when(jnp.logical_not(diagonal & (q == mine)))
        def _(q=q):
            f_out(q).start()

    @pl.when(diagonal)
    def _():
        frec[z] = fs[mine]

    for z_ in range(8):

        @pl.when(jnp.logical_not(diagonal & (z == z_)))
        def _(z_=z_):
            f_in(z_).wait_recv()

    total = frec[0]
    for z_ in range(1, 8):
        total = total + frec[z_]
    gv[...] = total * (1.0 / 24576.0**0.5)
    swap = rc(gv, gr, psend.at[3], precv.at[3], dev(c_=1 - c))
    swap.start()
    ov[pl.ds(pl.multiple_of(c * 32, 32), 32), :] = gv[...]
    swap.wait_recv()
    ov[pl.ds(pl.multiple_of((1 - c) * 32, 32), 32), :] = gr[...]
    ot[...] = ov[...].T
    of[...] = ot[pl.ds(pl.multiple_of(c * 64, 64), 64), :]
    result = pltpu.make_async_copy(of, out_hbm, lsem.at[7])
    result.start()

    swap.wait_send()
    m_pair(0).wait_send()
    m_pair(1).wait_send()
    for m in range(6):
        m_copy(m).wait_send()
    for d in (1, 2, 3):
        wy(0, q0, d, d).wait_send()
        wy(4, chunk(y, 4), d, d).wait_send()
    wz().wait_send()
    for q in range(8):

        @pl.when(jnp.logical_not(diagonal & (q == mine)))
        def _(q=q):
            f_out(q).wait_send()

    def drain(t, _):
        wp(t).wait_send()
        for m in range(6):
            x_copy(t, m).wait_send()
        for d in (1, 2, 3):
            z_copy(t, d).wait_send()
            y_copy(t, d).wait_send()
        return 0

    lax.fori_loop(0, CH, drain, 0)
    result.wait()


def on_device(samples, whitening, components):
    V = pltpu.VMEM
    D = pltpu.SemaphoreType.DMA
    scratch = [
        V((ROWS_DEV, FD), F32), V((64, 64), F32),
        V((ROWS_DEV, FD), BF16), V((ROWS_DEV, FD), BF16),
        V((CH, NC, 64, FD), F32), V((CH, 128, FD), BF16), V((CH, 128, FD), BF16),
        V((CH, 2, HB, 128), F32), V((CH, 2, 2, HB, 128), F32), V((CH, 2, HB, 128), F32),
        V((CH, 2, HB, 128), F32), V((CH, 2, 2, HB, 128), F32),
        V((CH, 4, SL, 128), F32), V((CH, 3, SL, 128), F32),
        V((CH, NY, SL, 128), F32), V((512, 1024), BF16), V((512, 1024), BF16),
        V((2, 32, 128), F32), V((32, 128), F32), V((2, 8, 4, 32, 128), F32),
        V((256, 1024), BF16), V((256, 1024), BF16),
        V((256, 512), F32), V((2, 128, 512), BF16), V((2, 128, 512), BF16),
        V((2, 2, 4, 4, 32, 128), F32), V((2, 4, 4, 32, 128), F32), V((4, 2, 4, 32, 128), F32),
        V((2, 4, 32, 128), F32), V((2, 2, 4, 32, 128), F32), V((8, 32, 128), F32), V((8, 32, 128), F32),
        V((32, 128), F32), V((32, 128), F32), V((64, 128), F32), V((128, 64), F32), V((64, 64), F32),
        D((8,)), D((8,)), D((8,)), D((8,)), D((8,)),
        D((8, 6)), D((8, 6)), D((8, 3)), D((8, 3)), D((8, 3)), D((8, 3)),
        D((5,)), D((5,)), D((2, 5)), D((2, 5)), D((4,)), D((4,)), D((6,)), D((6,)), D((8,)), D((8,)),
    ]
    return pl.pallas_call(
        kernel,
        out_shape=jax.ShapeDtypeStruct((64, 64), F32),
        in_specs=[pl.BlockSpec(memory_space=pl.ANY)] * 3,
        out_specs=pl.BlockSpec(memory_space=pl.ANY),
        scratch_shapes=scratch,
        compiler_params=pltpu.CompilerParams(
            collective_id=0, has_side_effects=True, vmem_limit_bytes=60 * 1024 * 1024
        ),
    )(samples, whitening.T, components)


def solution(mesh):
    placed = (P("rows", "feat"), P("feat", "rows"), P("rows", "feat"))
    return jax.shard_map(
        on_device, mesh=mesh, in_specs=placed, out_specs=P("rows", "feat"), check_vma=False
    )
```

```python
import jax
import jax.numpy as jnp
from jax import lax
from jax.experimental import pallas as pl
from jax.experimental.pallas import tpu as pltpu
from jax.sharding import PartitionSpec as P

MESH = pl.DeviceIdType.MESH
F32 = jnp.float32
BF16 = jnp.bfloat16
NX, NY, NZH, NZL, NC = 4, 4, 2, 4, 2
NZ = NZH * NZL
CH = NY * NZH
ROWS_DEV = 1536
BLK = ROWS_DEV // NX
ST = 2 * CH
HB = BLK // 4
SL = BLK // NZL // 2
FD = 512


def split(v):
    hi = v.astype(BF16)
    return hi, (v - hi.astype(F32)).astype(BF16)


def nt(a, b):
    return lax.dot_general(a, b, (((1,), (1,)), ((), ())), preferred_element_type=F32)


def nn(a, b):
    return lax.dot_general(a, b, (((1,), (0,)), ((), ())), preferred_element_type=F32)


def three(dot, ah, al, bh, bl):
    return dot(ah, bh) + (dot(ah, bl) + dot(al, bh))


def kernel(
    s_hbm, w_hbm, c_hbm, out_hbm,
    sv, cv, shi, slo, wall, whi, wlo,
    far, near, own, fr, nr, zb, zr, av, ahi, alo,
    ctp, cx, ct, chi, clo, pt, qhi, qlo, mb, mp, ms, mf, mr, fs, frec, gv, gr, ov, ot, of,
    lsem, wsend, wrecv, wpsend, wprecv, xsend, xrecv, zsend, zrecv, ysend, yrecv,
    csend, crecv, rsend, rrecv, psend, precv, msend, mrecv, fsend, frecv, tok_a, tok_b,
):
    i, j = lax.axis_index("rows"), lax.axis_index("feat")
    y, zh, c = i // 4, (i // 2) % 2, i % 2
    zl, x = j // 4, j % 4
    z = zh * 4 + zl
    xl, xr = (x + 3) % 4, (x + 1) % 4

    def dev(y_=None, zh_=None, c_=None, zl_=None, x_=None):
        y_ = y if y_ is None else y_
        zh_ = zh if zh_ is None else zh_
        c_ = c if c_ is None else c_
        zl_ = zl if zl_ is None else zl_
        x_ = x if x_ is None else x_
        return (y_ * 4 + zh_ * 2 + c_, zl_ * 4 + x_)

    def devz(z_, **kw):
        return dev(zh_=z_ // 4, zl_=z_ % 4, **kw)

    def rc(src, dst, ss, rs, to):
        return pltpu.make_async_remote_copy(
            src_ref=src, dst_ref=dst, send_sem=ss, recv_sem=rs, device_id=to, device_id_type=MESH
        )

    def chunk(y_, t):
        u = t % 4
        dy = u + (u // 2) * (1 - 2 * (u % 2))
        return ((y_ + dy) % 4) * 2 + (zh + t // 4) % 2

    q0 = chunk(y, 0)
    wcopy = pltpu.make_async_copy(w_hbm, wall.at[q0, c], lsem.at[0])
    ccopy = pltpu.make_async_copy(c_hbm, cv, lsem.at[1])
    wcopy.start()

    def scopy(d):
        rows = pl.ds(pl.multiple_of(((x + d) % 4) * BLK, BLK), BLK)
        return pltpu.make_async_copy(s_hbm.at[rows], sv.at[rows], lsem.at[2 + d])

    for d in (2, 1, 3, 0):
        scopy(d).start()
    ccopy.start()

    barrier = pltpu.get_barrier_semaphore()
    partners = [dev(x_=(x + d) % 4) for d in (1, 2, 3)]
    partners += [dev(y_=(y + d) % 4) for d in (1, 2, 3)]
    partners += [dev(zl_=(zl + d) % 4) for d in (1, 2, 3)]
    partners += [dev(zh_=1 - zh), dev(c_=1 - c), devz((z + 1) % 8), devz((z + 7) % 8)]
    for p in partners:
        pl.semaphore_signal(barrier, inc=1, device_id=p, device_id_type=MESH)

    wcopy.wait()
    pl.semaphore_wait(barrier, len(partners))

    def wy(base, q, d, t):
        return rc(wall.at[q, c], wall.at[q, c], wsend.at[base + d], wrecv.at[t], dev(y_=(y + d) % 4))

    def wz():
        return rc(wall.at[q0, c], wall.at[q0, c], wsend.at[4], wrecv.at[4], dev(zh_=1 - zh))

    def wp(t):
        q = chunk(y, t)
        return rc(wall.at[q, c], wall.at[q, c], wpsend.at[t], wprecv.at[t], dev(c_=1 - c))

    def w_arrived(t):
        q = chunk(y, t)
        rc(wall.at[q, c], wall.at[q, c], wsend.at[0], wrecv.at[t], dev(c_=1 - c)).wait_recv()

    def wp_arrived(t):
        q = chunk(y, t)
        rc(wall.at[q, c], wall.at[q, 1 - c], wpsend.at[t], wprecv.at[t], dev(c_=1 - c)).wait_recv()

    wp(0).start()
    wy(0, q0, 3, 1).start()
    wy(0, q0, 1, 2).start()
    wy(0, q0, 2, 3).start()
    wz().start()
    for d in (1, 2, 3):
        pl.semaphore_signal(tok_a, inc=1, device_id=dev(zl_=(zl + d) % 4), device_id_type=MESH)

    def split_s(d):
        scopy(d).wait()

        def body(n, _):
            rows = pl.ds(pl.multiple_of(((x + d) % 4) * BLK + n * 96, 96), 96)
            h, l = split(sv[rows, :])
            shi[rows, :] = h
            slo[rows, :] = l
            return 0

        lax.fori_loop(0, BLK // 96, body, 0)

    split_s(2)

    ccopy.wait()
    ct_own = cv[...].T
    cz = jnp.zeros((64, 64), F32)
    at0 = jnp.concatenate([ct_own, cz], axis=1)
    at1 = jnp.concatenate([cz, ct_own], axis=1)
    ctp[...] = jnp.where(c == 0, at0, at1).reshape(2, 32, 128)

    def c_swap():
        return rc(ctp.at[1 - c], cx, csend.at[0], crecv.at[0], dev(c_=1 - c))

    c_swap().start()
    qc = zl * 2 + zh

    def c_out(d):
        return rc(ctp.at[c], ct.at[c, y * 2 + zh, x], csend.at[1 + d], crecv.at[1 + x], dev(y_=zl, zl_=y, x_=d))

    def c_keep():
        return pltpu.make_async_copy(ctp.at[c], ct.at[c, y * 2 + zh, x], lsem.at[6])

    def c_in(d):
        return rc(ctp.at[c], ct.at[c, qc, d], csend.at[1 + d], crecv.at[1 + d], dev(y_=zl, zl_=y, x_=d))

    diagonal = y == zl

    def unit(z_):
        return ((z_ % 4) * 2 + z_ // 4) % 8

    def ring_r(k):
        q = unit((z + 9 - k) % 8)
        return rc(ct.at[c, q], ct.at[c, q], rsend.at[0, k], rrecv.at[0, k], devz((z + 1) % 8))

    def ring_l(k):
        q = unit((z + k + 7) % 8)
        return rc(ct.at[c, q], ct.at[c, q], rsend.at[1, k], rrecv.at[1, k], devz((z + 7) % 8))

    def ring_r_in(k):
        q = unit((z + 8 - k) % 8)
        return rc(ct.at[c, q], ct.at[c, q], rsend.at[0, k], rrecv.at[0, k], devz((z + 7) % 8))

    def ring_l_in(k):
        q = unit((z + k) % 8)
        return rc(ct.at[c, q], ct.at[c, q], rsend.at[1, k], rrecv.at[1, k], devz((z + 1) % 8))

    def c_pair():
        return rc(ct.at[c], ct.at[c], psend.at[0], precv.at[0], dev(c_=1 - c))

    def c_pair_in():
        return rc(ct.at[1 - c], ct.at[1 - c], psend.at[0], precv.at[0], dev(c_=1 - c))

    def block(t, d):
        rows = pl.ds(pl.multiple_of(((x + d) % 4) * BLK + (t % 2) * 2 * HB, 2 * HB), 2 * HB)
        return three(nt, shi[rows, :], slo[rows, :], whi[t // 2], wlo[t // 2]).reshape(2, HB, 128)

    def x_copy(t, m):
        src, dst, to = (
            (far.at[t, 0], fr.at[t, 0], xr),
            (far.at[t, 1], fr.at[t, 1], xl),
            (near.at[t, 0, 1], nr.at[t, 0, 1], xr),
            (near.at[t, 1, 0], nr.at[t, 1, 0], xl),
            (near.at[t, 0, 0], nr.at[t, 0, 0], xr),
            (near.at[t, 1, 1], nr.at[t, 1, 1], xl),
        )[m]
        return rc(src, dst, xsend.at[t, m], xrecv.at[t, m], dev(x_=to))

    def z_copy(t, d):
        return rc(zb.at[t, (zl + d) % 4], zr.at[t, d - 1], zsend.at[t, d - 1], zrecv.at[t, d - 1], dev(zl_=(zl + d) % 4))

    def y_copy(t, d):
        q = chunk(y, t // 2)
        h = t % 2
        return rc(av.at[q, y, h], av.at[q, y, h], ysend.at[t, d - 1], yrecv.at[t, d - 1], dev(y_=(y + d) % 4))

    def y_in(t, d):
        yo = (y + 4 - d) % 4
        q = chunk(yo, t // 2)
        h = t % 2
        return rc(av.at[q, yo, h], av.at[q, yo, h], ysend.at[t, d - 1], yrecv.at[t, d - 1], dev(y_=yo))

    def split_w(tc):
        q = chunk(y, tc)

        def body(n, _):
            h, l = split(wall[q, n])
            rows = pl.ds(pl.multiple_of(n * 64, 64), 64)
            whi[tc, rows, :] = h
            wlo[tc, rows, :] = l
            return 0

        lax.fori_loop(0, NC, body, 0)

    def far_step(t):
        far[t] = block(t, 2)
        x_copy(t, 0).start()
        x_copy(t, 1).start()

    def near_step(t):
        near[t, 0] = block(t, 1)
        x_copy(t, 2).start()
        near[t, 1] = block(t, 3)
        x_copy(t, 3).start()

    def join_step(t):
        for side in range(2):
            x_copy(t, side).wait_recv()
            near[t, side, side] = near[t, side, side] + fr[t, side]
            x_copy(t, 4 + side).start()

    def own_step(t):
        own[t] = block(t, 0)

    def x_finish(t):
        for m in range(2, 6):
            x_copy(t, m).wait_recv()
        for half in range(2):
            v = own[t, half] + nr[t, 0, half] + nr[t, 1, half]
            zb[t, 2 * half] = v[:SL]
            zb[t, 2 * half + 1] = v[SL:]
        for d in (2, 1, 3):
            z_copy(t, d).start()

    def keep(q, yo, h):
        hi, lo = split(av[q, yo, h])
        rows = pl.ds(pl.multiple_of(yo * 128 + h * SL, 16), SL)
        cols = pl.ds(pl.multiple_of(q * 128, 128), 128)
        ahi[rows, cols] = hi
        alo[rows, cols] = lo

    def z_finish(t):
        for d in (1, 2, 3):
            z_copy(t, d).wait_recv()
        q = chunk(y, t // 2)
        h = t % 2
        av[q, y, h] = (zb[t, zl] + zr[t, 0]) + (zr[t, 1] + zr[t, 2])
        for d in (2, 1, 3):
            y_copy(t, d).start()
        keep(q, y, h)

    def y_finish(t):
        for d in (1, 2, 3):
            y_in(t, d).wait_recv()
            yo = (y + 4 - d) % 4
            keep(chunk(yo, t // 2), yo, t % 2)

    for slot in range(NY):
        ahi[128 * slot + 2 * SL : 128 * slot + 128, :] = jnp.zeros((128 - 2 * SL, 1024), BF16)
        alo[128 * slot + 2 * SL : 128 * slot + 128, :] = jnp.zeros((128 - 2 * SL, 1024), BF16)
    wp_arrived(0)
    split_w(0)
    far_step(0)
    for d in (1, 3, 0):
        split_s(d)

    def whitening_step(t):
        @pl.when(t == 0)
        def _():
            w_arrived(1)
            wp(1).start()

        @pl.when(t < 6)
        def _():
            w_arrived(t + 2)
            wp(t + 2).start()

        @pl.when(t == 2)
        def _():
            q = chunk(y, 4)
            wy(4, q, 3, 5).start()
            wy(4, q, 1, 6).start()
            wy(4, q, 2, 7).start()

    def component_step(t):
        @pl.when(t == 0)
        def _():
            pl.semaphore_wait(tok_a, 3)
            for d in (1, 2, 3):
                pl.semaphore_signal(tok_b, inc=1, device_id=dev(x_=(x + d) % 4), device_id_type=MESH)

        @pl.when(t == 1)
        def _():
            pl.semaphore_wait(tok_b, 3)
            c_swap().wait()
            ctp[c] = ctp[c] + cx[...]
            for d in range(4):

                @pl.when(jnp.logical_not(diagonal & (x == d)))
                def _(d=d):
                    c_out(d).start()

            @pl.when(diagonal)
            def _():
                c_keep().start()
                c_keep().wait()

        @pl.when(t == 2)
        def _():
            for d in range(4):

                @pl.when(jnp.logical_not(diagonal & (x == d)))
                def _(d=d):
                    c_in(d).wait_recv()
                    c_out(d).wait_send()

            ring_r(1).start()
            ring_l(1).start()

        @pl.when((t >= 3) & (t < 7))
        def _():
            ring_r_in(t - 2).wait_recv()
            ring_r(t - 2).wait_send()

        @pl.when((t >= 3) & (t < 6))
        def _():
            ring_r(t - 1).start()
            ring_l_in(t - 2).wait_recv()
            ring_l(t - 2).wait_send()

        @pl.when((t >= 3) & (t < 5))
        def _():
            ring_l(t - 1).start()

        @pl.when(t == 6)
        def _():
            c_pair().start()

    def step(tc, _):
        for h in range(2):
            t = 2 * tc + h
            near_step(t)
            if h == 0:
                whitening_step(tc)
            join_step(t)
            if h == 0:
                far_step(t + 1)
                component_step(tc)
            else:

                @pl.when(tc < 7)
                def _():
                    wp_arrived(tc + 1)
                    split_w(tc + 1)
                    far_step(t + 1)

            own_step(t)

            @pl.when(t >= 2)
            def _():
                x_finish(t - 2)

            @pl.when(t >= 5)
            def _():
                z_finish(t - 5)

            @pl.when(t >= 8)
            def _():
                y_finish(t - 8)

        return 0

    def finish(what, lo, hi):
        def body(t, _):
            what(t)
            return 0

        lax.fori_loop(lo, hi, body, 0)

    lax.fori_loop(0, CH, step, 0)
    z_finish(11)
    x_finish(14)
    finish(z_finish, 12, 14)
    finish(y_finish, 8, 10)
    x_finish(15)
    z_finish(14)
    finish(y_finish, 10, 12)

    c_pair().wait_send()
    c_pair_in().wait_recv()

    def split_c(q, _):
        cols = pl.ds(pl.multiple_of(q * 128, 128), 128)
        for half in range(2):
            h, l = split(ct[half, q].reshape(128, 128))
            chi[128 * half : 128 * half + 128, cols] = h
            clo[128 * half : 128 * half + 128, cols] = l
        return 0

    lax.fori_loop(0, 8, split_c, 0)

    def project(t, d):
        yo = (y + 4 - d) % 4
        cols = pl.ds(pl.multiple_of(chunk(yo, t) * 128, 128), 128)
        slot = pl.ds(pl.multiple_of(yo * 128, 128), 128)
        pt[:, slot] = pt[:, slot] + three(nt, chi[:, cols], clo[:, cols], ahi[slot, cols], alo[slot, cols])

    def project_some(n, _):
        project(n // 4, n % 4)
        return 0

    pt[...] = jnp.zeros_like(pt)
    lax.fori_loop(0, 24, project_some, 0)
    finish(y_finish, 12, 14)
    lax.fori_loop(24, 28, project_some, 0)
    z_finish(15)
    lax.fori_loop(28, 29, project_some, 0)
    finish(y_finish, 14, 16)
    lax.fori_loop(29, 32, project_some, 0)

    h, l = split(pt[...] * pt[...])
    qhi[...] = h.reshape(2, 128, 512)
    qlo[...] = l.reshape(2, 128, 512)

    def moment_part(half, part):
        def body(n, _):
            cols = pl.ds(pl.multiple_of(part * 512 + n * 256, 256), 256)
            v = three(nn, qhi[half], qlo[half], ahi[:, cols], alo[:, cols])
            for u in range(2):
                mb[half, part, :, 2 * n + u] = v[:, 128 * u : 128 * u + 128].reshape(4, 32, 128)
            return 0

        lax.fori_loop(0, 2, body, 0)

    def m_pair(part):
        return rc(mb.at[1 - c, part], mp.at[part], psend.at[1 + part], precv.at[1 + part], dev(c_=1 - c))

    for part in range(2):
        moment_part(1 - c, part)
        m_pair(part).start()
    for part in range(2):
        moment_part(c, part)

    def m_copy(m):
        src, dst, to = (
            (ms.at[(x + 2) % 4, 0], mf.at[0], xr),
            (ms.at[(x + 2) % 4, 1], mf.at[1], xl),
            (ms.at[xr, 1], mr.at[0, 1], xr),
            (ms.at[xl, 0], mr.at[1, 0], xl),
            (ms.at[xr, 0], mr.at[0, 0], xr),
            (ms.at[xl, 1], mr.at[1, 1], xl),
        )[m]
        return rc(src, dst, msend.at[m], mrecv.at[m], dev(x_=to))

    def m_sum(b, part):
        ms[b, part] = mb[c, part, b] + mp[part, b]

    m_pair(0).wait_recv()
    m_sum((x + 2) % 4, 0)
    m_copy(0).start()
    m_sum(xl, 0)
    m_copy(3).start()
    m_pair(1).wait_recv()
    m_sum((x + 2) % 4, 1)
    m_copy(1).start()
    m_sum(xr, 1)
    m_copy(2).start()
    m_sum(xr, 0)
    m_copy(0).wait_recv()
    ms[xr, 0] = ms[xr, 0] + mf[0]
    m_copy(4).start()
    m_sum(xl, 1)
    m_copy(1).wait_recv()
    ms[xl, 1] = ms[xl, 1] + mf[1]
    m_copy(5).start()
    m_sum(x, 0)
    m_sum(x, 1)
    for m in range(2, 6):
        m_copy(m).wait_recv()
    fs[...] = ms[x].reshape(8, 32, 128) + (mr[0] + mr[1]).reshape(8, 32, 128)

    def f_out(q):
        return rc(fs.at[q], frec.at[z], fsend.at[q], frecv.at[z], dev(y_=q // 2, zh_=q % 2, zl_=y))

    def f_in(z_):
        return rc(fs.at[0], frec.at[z_], fsend.at[0], frecv.at[z_], devz(z_, y_=zl))

    mine = y * 2 + zh
    for q in range(8):

        @pl.when(jnp.logical_not(diagonal & (q == mine)))
        def _(q=q):
            f_out(q).start()

    @pl.when(diagonal)
    def _():
        frec[z] = fs[mine]

    for z_ in range(8):

        @pl.when(jnp.logical_not(diagonal & (z == z_)))
        def _(z_=z_):
            f_in(z_).wait_recv()

    total = frec[0]
    for z_ in range(1, 8):
        total = total + frec[z_]
    gv[...] = total * (1.0 / 24576.0**0.5)
    swap = rc(gv, gr, psend.at[3], precv.at[3], dev(c_=1 - c))
    swap.start()
    ov[pl.ds(pl.multiple_of(c * 32, 32), 32), :] = gv[...]
    swap.wait_recv()
    ov[pl.ds(pl.multiple_of((1 - c) * 32, 32), 32), :] = gr[...]
    ot[...] = ov[...].T
    of[...] = ot[pl.ds(pl.multiple_of(c * 64, 64), 64), :]
    result = pltpu.make_async_copy(of, out_hbm, lsem.at[7])
    result.start()

    swap.wait_send()
    m_pair(0).wait_send()
    m_pair(1).wait_send()
    for m in range(6):
        m_copy(m).wait_send()
    for d in (1, 2, 3):
        wy(0, q0, d, d).wait_send()
        wy(4, chunk(y, 4), d, d).wait_send()
    wz().wait_send()
    for q in range(8):

        @pl.when(jnp.logical_not(diagonal & (q == mine)))
        def _(q=q):
            f_out(q).wait_send()

    def drain_w(t, _):
        wp(t).wait_send()
        return 0

    lax.fori_loop(0, CH, drain_w, 0)

    def drain(t, _):
        for m in range(6):
            x_copy(t, m).wait_send()
        for d in (1, 2, 3):
            z_copy(t, d).wait_send()
            y_copy(t, d).wait_send()
        return 0

    lax.fori_loop(0, ST, drain, 0)
    result.wait()


def on_device(samples, whitening, components):
    V = pltpu.VMEM
    D = pltpu.SemaphoreType.DMA
    scratch = [
        V((ROWS_DEV, FD), F32), V((64, 64), F32),
        V((ROWS_DEV, FD), BF16), V((ROWS_DEV, FD), BF16),
        V((CH, NC, 64, FD), F32), V((CH, 128, FD), BF16), V((CH, 128, FD), BF16),
        V((ST, 2, HB, 128), F32), V((ST, 2, 2, HB, 128), F32), V((ST, 2, HB, 128), F32),
        V((ST, 2, HB, 128), F32), V((ST, 2, 2, HB, 128), F32),
        V((ST, 4, SL, 128), F32), V((ST, 3, SL, 128), F32),
        V((CH, NY, 2, SL, 128), F32), V((512, 1024), BF16), V((512, 1024), BF16),
        V((2, 32, 128), F32), V((32, 128), F32), V((2, 8, 4, 32, 128), F32),
        V((256, 1024), BF16), V((256, 1024), BF16),
        V((256, 512), F32), V((2, 128, 512), BF16), V((2, 128, 512), BF16),
        V((2, 2, 4, 4, 32, 128), F32), V((2, 4, 4, 32, 128), F32), V((4, 2, 4, 32, 128), F32),
        V((2, 4, 32, 128), F32), V((2, 2, 4, 32, 128), F32), V((8, 32, 128), F32), V((8, 32, 128), F32),
        V((32, 128), F32), V((32, 128), F32), V((64, 128), F32), V((128, 64), F32), V((64, 64), F32),
        D((8,)), D((8,)), D((8,)), D((8,)), D((8,)),
        D((ST, 6)), D((ST, 6)), D((ST, 3)), D((ST, 3)), D((ST, 3)), D((ST, 3)),
        D((5,)), D((5,)), D((2, 5)), D((2, 5)), D((4,)), D((4,)), D((6,)), D((6,)), D((8,)), D((8,)),
        pltpu.SemaphoreType.REGULAR, pltpu.SemaphoreType.REGULAR,
    ]
    return pl.pallas_call(
        kernel,
        out_shape=jax.ShapeDtypeStruct((64, 64), F32),
        in_specs=[pl.BlockSpec(memory_space=pl.ANY)] * 3,
        out_specs=pl.BlockSpec(memory_space=pl.ANY),
        scratch_shapes=scratch,
        compiler_params=pltpu.CompilerParams(
            collective_id=0, has_side_effects=True, vmem_limit_bytes=60 * 1024 * 1024
        ),
    )(samples, whitening.T, components)


def solution(mesh):
    placed = (P("rows", "feat"), P("feat", "rows"), P("rows", "feat"))
    return jax.shard_map(
        on_device, mesh=mesh, in_specs=placed, out_specs=P("rows", "feat"), check_vma=False
    )
```

```python
import jax
import jax.numpy as jnp
from jax import lax
from jax.experimental import pallas as pl
from jax.experimental.pallas import tpu as pltpu
from jax.sharding import PartitionSpec as P

MESH = pl.DeviceIdType.MESH
F32 = jnp.float32
BF16 = jnp.bfloat16
NX, NY, NZH, NZL, NC = 4, 4, 2, 4, 2
NZ = NZH * NZL
CH = NY * NZH
ROWS_DEV = 1536
BLK = ROWS_DEV // NX
HB = BLK // 2
SL = BLK // NZL
FD = 512


def split(v):
    hi = v.astype(BF16)
    return hi, (v - hi.astype(F32)).astype(BF16)


def nt(a, b):
    return lax.dot_general(a, b, (((1,), (1,)), ((), ())), preferred_element_type=F32)


def nn(a, b):
    return lax.dot_general(a, b, (((1,), (0,)), ((), ())), preferred_element_type=F32)


def three(dot, ah, al, bh, bl):
    return dot(ah, bh) + (dot(ah, bl) + dot(al, bh))


def kernel(
    s_hbm, w_hbm, c_hbm, out_hbm,
    sv, cv, shi, slo, wall, whi, wlo,
    far, near, own, fr, nr, zb, zr, av, ahi, alo,
    ctp, cx, ct, chi, clo, pt, qhi, qlo, mb, mp, ms, mf, mr, fs, frec, gv, gr, ov, ot, of,
    lsem, wsend, wrecv, wpsend, wprecv, xsend, xrecv, zsend, zrecv, ysend, yrecv,
    csend, crecv, rsend, rrecv, psend, precv, msend, mrecv, fsend, frecv, tok_a, tok_b,
):
    i, j = lax.axis_index("rows"), lax.axis_index("feat")
    y, zh, c = i // 4, (i // 2) % 2, i % 2
    zl, x = j // 4, j % 4
    z = zh * 4 + zl
    xl, xr = (x + 3) % 4, (x + 1) % 4

    def dev(y_=None, zh_=None, c_=None, zl_=None, x_=None):
        y_ = y if y_ is None else y_
        zh_ = zh if zh_ is None else zh_
        c_ = c if c_ is None else c_
        zl_ = zl if zl_ is None else zl_
        x_ = x if x_ is None else x_
        return (y_ * 4 + zh_ * 2 + c_, zl_ * 4 + x_)

    def devz(z_, **kw):
        return dev(zh_=z_ // 4, zl_=z_ % 4, **kw)

    def rc(src, dst, ss, rs, to):
        return pltpu.make_async_remote_copy(
            src_ref=src, dst_ref=dst, send_sem=ss, recv_sem=rs, device_id=to, device_id_type=MESH
        )

    def chunk(y_, t):
        u = t % 4
        dy = u + (u // 2) * (1 - 2 * (u % 2))
        return ((y_ + dy) % 4) * 2 + (zh + t // 4) % 2

    q0 = chunk(y, 0)
    wcopy = pltpu.make_async_copy(w_hbm, wall.at[q0, c], lsem.at[0])
    ccopy = pltpu.make_async_copy(c_hbm, cv, lsem.at[1])
    wcopy.start()

    def scopy(d):
        rows = pl.ds(pl.multiple_of(((x + d) % 4) * BLK, BLK), BLK)
        return pltpu.make_async_copy(s_hbm.at[rows], sv.at[rows], lsem.at[2 + d])

    for d in (2, 1, 3, 0):
        scopy(d).start()
    ccopy.start()

    barrier = pltpu.get_barrier_semaphore()
    partners = [dev(x_=(x + d) % 4) for d in (1, 2, 3)]
    partners += [dev(y_=(y + d) % 4) for d in (1, 2, 3)]
    partners += [dev(zl_=(zl + d) % 4) for d in (1, 2, 3)]
    partners += [dev(zh_=1 - zh), dev(c_=1 - c), devz((z + 1) % 8), devz((z + 7) % 8)]
    for p in partners:
        pl.semaphore_signal(barrier, inc=1, device_id=p, device_id_type=MESH)

    wcopy.wait()
    pl.semaphore_wait(barrier, len(partners))

    def wy(base, q, d, t):
        return rc(wall.at[q, c], wall.at[q, c], wsend.at[base + d], wrecv.at[t], dev(y_=(y + d) % 4))

    def wz():
        return rc(wall.at[q0, c], wall.at[q0, c], wsend.at[4], wrecv.at[4], dev(zh_=1 - zh))

    def wp(t):
        q = chunk(y, t)
        return rc(wall.at[q, c], wall.at[q, c], wpsend.at[t], wprecv.at[t], dev(c_=1 - c))

    def w_arrived(t):
        q = chunk(y, t)
        rc(wall.at[q, c], wall.at[q, c], wsend.at[0], wrecv.at[t], dev(c_=1 - c)).wait_recv()

    def wp_arrived(t):
        q = chunk(y, t)
        rc(wall.at[q, c], wall.at[q, 1 - c], wpsend.at[t], wprecv.at[t], dev(c_=1 - c)).wait_recv()

    wp(0).start()
    wy(0, q0, 3, 1).start()
    wy(0, q0, 1, 2).start()
    wy(0, q0, 2, 3).start()
    wz().start()
    for d in (1, 2, 3):
        pl.semaphore_signal(tok_a, inc=1, device_id=dev(zl_=(zl + d) % 4), device_id_type=MESH)

    def split_s(d):
        scopy(d).wait()

        def body(n, _):
            rows = pl.ds(pl.multiple_of(((x + d) % 4) * BLK + n * 96, 96), 96)
            h, l = split(sv[rows, :])
            shi[rows, :] = h
            slo[rows, :] = l
            return 0

        lax.fori_loop(0, BLK // 96, body, 0)

    split_s(2)

    ccopy.wait()
    ct_own = cv[...].T
    cz = jnp.zeros((64, 64), F32)
    at0 = jnp.concatenate([ct_own, cz], axis=1)
    at1 = jnp.concatenate([cz, ct_own], axis=1)
    ctp[...] = jnp.where(c == 0, at0, at1).reshape(2, 32, 128)

    def c_swap():
        return rc(ctp.at[1 - c], cx, csend.at[0], crecv.at[0], dev(c_=1 - c))

    c_swap().start()
    qc = zl * 2 + zh

    def c_out(d):
        return rc(ctp.at[c], ct.at[c, y * 2 + zh, x], csend.at[1 + d], crecv.at[1 + x], dev(y_=zl, zl_=y, x_=d))

    def c_keep():
        return pltpu.make_async_copy(ctp.at[c], ct.at[c, y * 2 + zh, x], lsem.at[6])

    def c_in(d):
        return rc(ctp.at[c], ct.at[c, qc, d], csend.at[1 + d], crecv.at[1 + d], dev(y_=zl, zl_=y, x_=d))

    diagonal = y == zl

    def unit(z_):
        return ((z_ % 4) * 2 + z_ // 4) % 8

    def ring_r(k):
        q = unit((z + 9 - k) % 8)
        return rc(ct.at[c, q], ct.at[c, q], rsend.at[0, k], rrecv.at[0, k], devz((z + 1) % 8))

    def ring_l(k):
        q = unit((z + k + 7) % 8)
        return rc(ct.at[c, q], ct.at[c, q], rsend.at[1, k], rrecv.at[1, k], devz((z + 7) % 8))

    def ring_r_in(k):
        q = unit((z + 8 - k) % 8)
        return rc(ct.at[c, q], ct.at[c, q], rsend.at[0, k], rrecv.at[0, k], devz((z + 7) % 8))

    def ring_l_in(k):
        q = unit((z + k) % 8)
        return rc(ct.at[c, q], ct.at[c, q], rsend.at[1, k], rrecv.at[1, k], devz((z + 1) % 8))

    def c_pair():
        return rc(ct.at[c], ct.at[c], psend.at[0], precv.at[0], dev(c_=1 - c))

    def c_pair_in():
        return rc(ct.at[1 - c], ct.at[1 - c], psend.at[0], precv.at[0], dev(c_=1 - c))

    def block(t, d):
        rows = pl.ds(pl.multiple_of(((x + d) % 4) * BLK, BLK), BLK)
        return three(nt, shi[rows, :], slo[rows, :], whi[t], wlo[t])

    def x_copy(t, m):
        src, dst, to = (
            (far.at[t, 0], fr.at[t, 0], xr),
            (far.at[t, 1], fr.at[t, 1], xl),
            (near.at[t, 0, 1], nr.at[t, 0, 1], xr),
            (near.at[t, 1, 0], nr.at[t, 1, 0], xl),
            (near.at[t, 0, 0], nr.at[t, 0, 0], xr),
            (near.at[t, 1, 1], nr.at[t, 1, 1], xl),
        )[m]
        return rc(src, dst, xsend.at[t, m], xrecv.at[t, m], dev(x_=to))

    def z_copy(t, d):
        return rc(zb.at[t, (zl + d) % 4], zr.at[t, d - 1], zsend.at[t, d - 1], zrecv.at[t, d - 1], dev(zl_=(zl + d) % 4))

    def y_copy(t, d):
        q = chunk(y, t)
        return rc(av.at[q, y], av.at[q, y], ysend.at[t, d - 1], yrecv.at[t, d - 1], dev(y_=(y + d) % 4))

    def y_in(t, d):
        yo = (y + 4 - d) % 4
        q = chunk(yo, t)
        return rc(av.at[q, yo], av.at[q, yo], ysend.at[t, d - 1], yrecv.at[t, d - 1], dev(y_=yo))

    def split_w(t):
        q = chunk(y, t)

        def body(n, _):
            h, l = split(wall[q, n])
            rows = pl.ds(pl.multiple_of(n * 64, 64), 64)
            whi[t, rows, :] = h
            wlo[t, rows, :] = l
            return 0

        lax.fori_loop(0, NC, body, 0)

    def far_step(t):
        far[t] = block(t, 2).reshape(2, HB, 128)
        x_copy(t, 0).start()
        x_copy(t, 1).start()

    def near_step(t):
        near[t, 0] = block(t, 1).reshape(2, HB, 128)
        x_copy(t, 2).start()
        near[t, 1] = block(t, 3).reshape(2, HB, 128)
        x_copy(t, 3).start()

    def join_step(t):
        for side in range(2):
            x_copy(t, side).wait_recv()
            near[t, side, side] = near[t, side, side] + fr[t, side]
            x_copy(t, 4 + side).start()

    def own_step(t):
        own[t] = block(t, 0).reshape(2, HB, 128)

    def x_finish(t):
        for m in range(2, 6):
            x_copy(t, m).wait_recv()
        for half in range(2):
            v = own[t, half] + nr[t, 0, half] + nr[t, 1, half]
            zb[t, 2 * half] = v[:SL]
            zb[t, 2 * half + 1] = v[SL:]
        for d in (2, 1, 3):
            z_copy(t, d).start()

    def keep(q, yo):
        h, l = split(av[q, yo])
        rows = pl.ds(pl.multiple_of(yo * 128, 128), SL)
        cols = pl.ds(pl.multiple_of(q * 128, 128), 128)
        ahi[rows, cols] = h
        alo[rows, cols] = l

    def z_finish(t):
        for d in (1, 2, 3):
            z_copy(t, d).wait_recv()
        q = chunk(y, t)
        av[q, y] = (zb[t, zl] + zr[t, 0]) + (zr[t, 1] + zr[t, 2])
        for d in (2, 1, 3):
            y_copy(t, d).start()
        keep(q, y)

    def y_finish(t):
        for d in (1, 2, 3):
            y_in(t, d).wait_recv()
            yo = (y + 4 - d) % 4
            keep(chunk(yo, t), yo)

    for slot in range(NY):
        ahi[128 * slot + SL : 128 * slot + 128, :] = jnp.zeros((128 - SL, 1024), BF16)
        alo[128 * slot + SL : 128 * slot + 128, :] = jnp.zeros((128 - SL, 1024), BF16)
    wp_arrived(0)
    split_w(0)
    far_step(0)
    for d in (1, 3, 0):
        split_s(d)
    near_step(0)
    w_arrived(1)
    wp(1).start()
    w_arrived(2)
    wp(2).start()
    wp_arrived(1)
    split_w(1)
    far_step(1)

    def step(t, _):
        join_step(t)

        @pl.when(t == 0)
        def _():
            w_arrived(3)
            wp(3).start()

        @pl.when(t == 1)
        def _():
            w_arrived(4)
            q = chunk(y, 4)
            wp(4).start()
            wy(4, q, 3, 5).start()
            wy(4, q, 1, 6).start()
            wy(4, q, 2, 7).start()

        @pl.when((t >= 2) & (t < 5))
        def _():
            w_arrived(t + 3)
            wp(t + 3).start()

        @pl.when(t < 7)
        def _():
            near_step(t + 1)

        @pl.when(t < 6)
        def _():
            wp_arrived(t + 2)
            split_w(t + 2)
            far_step(t + 2)

        @pl.when(t == 0)
        def _():
            pl.semaphore_wait(tok_a, 3)
            for d in (1, 2, 3):
                pl.semaphore_signal(tok_b, inc=1, device_id=dev(x_=(x + d) % 4), device_id_type=MESH)

        @pl.when(t == 1)
        def _():
            pl.semaphore_wait(tok_b, 3)
            c_swap().wait()
            ctp[c] = ctp[c] + cx[...]
            for d in range(4):

                @pl.when(jnp.logical_not(diagonal & (x == d)))
                def _(d=d):
                    c_out(d).start()

            @pl.when(diagonal)
            def _():
                c_keep().start()
                c_keep().wait()

        @pl.when(t == 2)
        def _():
            for d in range(4):

                @pl.when(jnp.logical_not(diagonal & (x == d)))
                def _(d=d):
                    c_in(d).wait_recv()
                    c_out(d).wait_send()

            ring_r(1).start()
            ring_l(1).start()

        @pl.when((t >= 3) & (t < 7))
        def _():
            ring_r_in(t - 2).wait_recv()
            ring_r(t - 2).wait_send()

        @pl.when((t >= 3) & (t < 6))
        def _():
            ring_r(t - 1).start()
            ring_l_in(t - 2).wait_recv()
            ring_l(t - 2).wait_send()

        @pl.when((t >= 3) & (t < 5))
        def _():
            ring_l(t - 1).start()

        @pl.when(t == 6)
        def _():
            c_pair().start()

        own_step(t)

        @pl.when(t >= 1)
        def _():
            x_finish(t - 1)

        @pl.when(t >= 3)
        def _():
            z_finish(t - 3)

        @pl.when(t >= 5)
        def _():
            y_finish(t - 5)

        return 0

    lax.fori_loop(0, CH, step, 0)
    z_finish(5)
    c_pair().wait_send()
    c_pair_in().wait_recv()

    def split_c(q, _):
        cols = pl.ds(pl.multiple_of(q * 128, 128), 128)
        for half in range(2):
            h, l = split(ct[half, q].reshape(128, 128))
            chi[128 * half : 128 * half + 128, cols] = h
            clo[128 * half : 128 * half + 128, cols] = l
        return 0

    lax.fori_loop(0, 8, split_c, 0)

    def project(t, d):
        yo = (y + 4 - d) % 4
        cols = pl.ds(pl.multiple_of(chunk(yo, t) * 128, 128), 128)
        slot = pl.ds(pl.multiple_of(yo * 128, 128), 128)
        pt[:, slot] = pt[:, slot] + three(nt, chi[:, cols], clo[:, cols], ahi[slot, cols], alo[slot, cols])

    def project_some(n, _):
        project(n // 4, n % 4)
        return 0

    pt[...] = jnp.zeros_like(pt)
    lax.fori_loop(0, 4, project_some, 0)
    x_finish(7)
    z_finish(6)
    y_finish(3)
    y_finish(4)
    lax.fori_loop(4, 20, project_some, 0)
    y_finish(5)
    lax.fori_loop(20, 24, project_some, 0)
    z_finish(7)
    y_finish(6)
    lax.fori_loop(24, 29, project_some, 0)
    y_finish(7)
    lax.fori_loop(29, 32, project_some, 0)

    h, l = split(pt[...] * pt[...])
    qhi[...] = h.reshape(2, 128, 512)
    qlo[...] = l.reshape(2, 128, 512)

    def moment_part(half, part):
        def body(n, _):
            cols = pl.ds(pl.multiple_of(part * 512 + n * 256, 256), 256)
            v = three(nn, qhi[half], qlo[half], ahi[:, cols], alo[:, cols])
            for u in range(2):
                mb[half, part, :, 2 * n + u] = v[:, 128 * u : 128 * u + 128].reshape(4, 32, 128)
            return 0

        lax.fori_loop(0, 2, body, 0)

    def m_pair(part):
        return rc(mb.at[1 - c, part], mp.at[part], psend.at[1 + part], precv.at[1 + part], dev(c_=1 - c))

    for part in range(2):
        moment_part(1 - c, part)
        m_pair(part).start()
    for part in range(2):
        moment_part(c, part)

    def m_copy(m):
        src, dst, to = (
            (ms.at[(x + 2) % 4, 0], mf.at[0], xr),
            (ms.at[(x + 2) % 4, 1], mf.at[1], xl),
            (ms.at[xr, 1], mr.at[0, 1], xr),
            (ms.at[xl, 0], mr.at[1, 0], xl),
            (ms.at[xr, 0], mr.at[0, 0], xr),
            (ms.at[xl, 1], mr.at[1, 1], xl),
        )[m]
        return rc(src, dst, msend.at[m], mrecv.at[m], dev(x_=to))

    def m_sum(b, part):
        ms[b, part] = mb[c, part, b] + mp[part, b]

    m_pair(0).wait_recv()
    m_sum((x + 2) % 4, 0)
    m_copy(0).start()
    m_sum(xl, 0)
    m_copy(3).start()
    m_pair(1).wait_recv()
    m_sum((x + 2) % 4, 1)
    m_copy(1).start()
    m_sum(xr, 1)
    m_copy(2).start()
    m_sum(xr, 0)
    m_copy(0).wait_recv()
    ms[xr, 0] = ms[xr, 0] + mf[0]
    m_copy(4).start()
    m_sum(xl, 1)
    m_copy(1).wait_recv()
    ms[xl, 1] = ms[xl, 1] + mf[1]
    m_copy(5).start()
    m_sum(x, 0)
    m_sum(x, 1)
    def f_out(q):
        return rc(fs.at[q], frec.at[z], fsend.at[q], frecv.at[z], dev(y_=q // 2, zh_=q % 2, zl_=y))

    def f_in(z_):
        return rc(fs.at[0], frec.at[z_], fsend.at[0], frecv.at[z_], devz(z_, y_=zl))

    mine = y * 2 + zh
    for part in range(2):
        m_copy(3 - part).wait_recv()
        m_copy(4 + part).wait_recv()
        fs[4 * part : 4 * part + 4] = ms[x, part] + (mr[0, part] + mr[1, part])
        for q in range(4 * part, 4 * part + 4):

            @pl.when(jnp.logical_not(diagonal & (q == mine)))
            def _(q=q):
                f_out(q).start()

    @pl.when(diagonal)
    def _():
        frec[z] = fs[mine]

    for z_ in range(8):

        @pl.when(jnp.logical_not(diagonal & (z == z_)))
        def _(z_=z_):
            f_in(z_).wait_recv()

    total = frec[0]
    for z_ in range(1, 8):
        total = total + frec[z_]
    gv[...] = total * (1.0 / 24576.0**0.5)
    swap = rc(gv, gr, psend.at[3], precv.at[3], dev(c_=1 - c))
    swap.start()
    ov[pl.ds(pl.multiple_of(c * 32, 32), 32), :] = gv[...]
    swap.wait_recv()
    ov[pl.ds(pl.multiple_of((1 - c) * 32, 32), 32), :] = gr[...]
    ot[...] = ov[...].T
    of[...] = ot[pl.ds(pl.multiple_of(c * 64, 64), 64), :]
    result = pltpu.make_async_copy(of, out_hbm, lsem.at[7])
    result.start()

    swap.wait_send()
    m_pair(0).wait_send()
    m_pair(1).wait_send()
    for m in range(6):
        m_copy(m).wait_send()
    for d in (1, 2, 3):
        wy(0, q0, d, d).wait_send()
        wy(4, chunk(y, 4), d, d).wait_send()
    wz().wait_send()
    for q in range(8):

        @pl.when(jnp.logical_not(diagonal & (q == mine)))
        def _(q=q):
            f_out(q).wait_send()

    def drain(t, _):
        wp(t).wait_send()
        for m in range(6):
            x_copy(t, m).wait_send()
        for d in (1, 2, 3):
            z_copy(t, d).wait_send()
            y_copy(t, d).wait_send()
        return 0

    lax.fori_loop(0, CH, drain, 0)
    result.wait()


def on_device(samples, whitening, components):
    V = pltpu.VMEM
    D = pltpu.SemaphoreType.DMA
    scratch = [
        V((ROWS_DEV, FD), F32), V((64, 64), F32),
        V((ROWS_DEV, FD), BF16), V((ROWS_DEV, FD), BF16),
        V((CH, NC, 64, FD), F32), V((CH, 128, FD), BF16), V((CH, 128, FD), BF16),
        V((CH, 2, HB, 128), F32), V((CH, 2, 2, HB, 128), F32), V((CH, 2, HB, 128), F32),
        V((CH, 2, HB, 128), F32), V((CH, 2, 2, HB, 128), F32),
        V((CH, 4, SL, 128), F32), V((CH, 3, SL, 128), F32),
        V((CH, NY, SL, 128), F32), V((512, 1024), BF16), V((512, 1024), BF16),
        V((2, 32, 128), F32), V((32, 128), F32), V((2, 8, 4, 32, 128), F32),
        V((256, 1024), BF16), V((256, 1024), BF16),
        V((256, 512), F32), V((2, 128, 512), BF16), V((2, 128, 512), BF16),
        V((2, 2, 4, 4, 32, 128), F32), V((2, 4, 4, 32, 128), F32), V((4, 2, 4, 32, 128), F32),
        V((2, 4, 32, 128), F32), V((2, 2, 4, 32, 128), F32), V((8, 32, 128), F32), V((8, 32, 128), F32),
        V((32, 128), F32), V((32, 128), F32), V((64, 128), F32), V((128, 64), F32), V((64, 64), F32),
        D((8,)), D((8,)), D((8,)), D((8,)), D((8,)),
        D((8, 6)), D((8, 6)), D((8, 3)), D((8, 3)), D((8, 3)), D((8, 3)),
        D((5,)), D((5,)), D((2, 5)), D((2, 5)), D((4,)), D((4,)), D((6,)), D((6,)), D((8,)), D((8,)),
        pltpu.SemaphoreType.REGULAR, pltpu.SemaphoreType.REGULAR,
    ]
    return pl.pallas_call(
        kernel,
        out_shape=jax.ShapeDtypeStruct((64, 64), F32),
        in_specs=[pl.BlockSpec(memory_space=pl.ANY)] * 3,
        out_specs=pl.BlockSpec(memory_space=pl.ANY),
        scratch_shapes=scratch,
        compiler_params=pltpu.CompilerParams(
            collective_id=0, has_side_effects=True, vmem_limit_bytes=60 * 1024 * 1024
        ),
    )(samples, whitening.T, components)


def solution(mesh):
    placed = (P("rows", "feat"), P("feat", "rows"), P("rows", "feat"))
    return jax.shard_map(
        on_device, mesh=mesh, in_specs=placed, out_specs=P("rows", "feat"), check_vma=False
    )
```

```python
import jax
import jax.numpy as jnp
from jax import lax
from jax.experimental import pallas as pl
from jax.experimental.pallas import tpu as pltpu
from jax.sharding import PartitionSpec as P

MESH = pl.DeviceIdType.MESH
F32 = jnp.float32
BF16 = jnp.bfloat16
NX, NY, NZH, NZL, NC = 4, 4, 2, 4, 2
NZ = NZH * NZL
CH = NY * NZH
ROWS_DEV = 1536
BLK = ROWS_DEV // NX
HB = BLK // 2
SL = BLK // NZL
FD = 512


def split(v):
    hi = v.astype(BF16)
    return hi, (v - hi.astype(F32)).astype(BF16)


def nt(a, b):
    return lax.dot_general(a, b, (((1,), (1,)), ((), ())), preferred_element_type=F32)


def nn(a, b):
    return lax.dot_general(a, b, (((1,), (0,)), ((), ())), preferred_element_type=F32)


def three(dot, ah, al, bh, bl):
    return dot(ah, bh) + (dot(ah, bl) + dot(al, bh))


def kernel(
    s_hbm, w_hbm, c_hbm, out_hbm,
    sv, cv, shi, slo, wall, whi, wlo,
    far, near, own, fr, nr, zb, zr, av, ahi, alo,
    ctp, cx, ct, chi, clo, pt, qhi, qlo, mb, mp, ms, mf, mr, fs, frec, gv, gr, ov, ot, of,
    lsem, wsend, wrecv, wpsend, wprecv, xsend, xrecv, zsend, zrecv, ysend, yrecv,
    csend, crecv, rsend, rrecv, psend, precv, msend, mrecv, fsend, frecv, tok_a, tok_b,
):
    i, j = lax.axis_index("rows"), lax.axis_index("feat")
    y, zh, c = i // 4, (i // 2) % 2, i % 2
    zl, x = j // 4, j % 4
    z = zh * 4 + zl
    xl, xr = (x + 3) % 4, (x + 1) % 4

    def dev(y_=None, zh_=None, c_=None, zl_=None, x_=None):
        y_ = y if y_ is None else y_
        zh_ = zh if zh_ is None else zh_
        c_ = c if c_ is None else c_
        zl_ = zl if zl_ is None else zl_
        x_ = x if x_ is None else x_
        return (y_ * 4 + zh_ * 2 + c_, zl_ * 4 + x_)

    def devz(z_, **kw):
        return dev(zh_=z_ // 4, zl_=z_ % 4, **kw)

    def rc(src, dst, ss, rs, to):
        return pltpu.make_async_remote_copy(
            src_ref=src, dst_ref=dst, send_sem=ss, recv_sem=rs, device_id=to, device_id_type=MESH
        )

    def chunk(y_, t):
        u = t % 4
        dy = u + (u // 2) * (1 - 2 * (u % 2))
        return ((y_ + dy) % 4) * 2 + (zh + t // 4) % 2

    q0 = chunk(y, 0)
    wcopy = pltpu.make_async_copy(w_hbm, wall.at[q0, c], lsem.at[0])
    ccopy = pltpu.make_async_copy(c_hbm, cv, lsem.at[1])
    wcopy.start()

    def scopy(d):
        rows = pl.ds(pl.multiple_of(((x + d) % 4) * BLK, BLK), BLK)
        return pltpu.make_async_copy(s_hbm.at[rows], sv.at[rows], lsem.at[2 + d])

    for d in (2, 1, 3, 0):
        scopy(d).start()
    ccopy.start()

    barrier = pltpu.get_barrier_semaphore()
    partners = [dev(x_=(x + d) % 4) for d in (1, 2, 3)]
    partners += [dev(y_=(y + d) % 4) for d in (1, 2, 3)]
    partners += [dev(zl_=(zl + d) % 4) for d in (1, 2, 3)]
    partners += [dev(zh_=1 - zh), dev(c_=1 - c), devz((z + 1) % 8), devz((z + 7) % 8)]
    for p in partners:
        pl.semaphore_signal(barrier, inc=1, device_id=p, device_id_type=MESH)

    wcopy.wait()
    pl.semaphore_wait(barrier, len(partners))

    def wy(base, q, d, t):
        return rc(wall.at[q, c], wall.at[q, c], wsend.at[base + d], wrecv.at[t], dev(y_=(y + d) % 4))

    def wz():
        return rc(wall.at[q0, c], wall.at[q0, c], wsend.at[4], wrecv.at[4], dev(zh_=1 - zh))

    def wp(t):
        q = chunk(y, t)
        return rc(wall.at[q, c], wall.at[q, c], wpsend.at[t], wprecv.at[t], dev(c_=1 - c))

    def w_arrived(t):
        q = chunk(y, t)
        rc(wall.at[q, c], wall.at[q, c], wsend.at[0], wrecv.at[t], dev(c_=1 - c)).wait_recv()

    def wp_arrived(t):
        q = chunk(y, t)
        rc(wall.at[q, c], wall.at[q, 1 - c], wpsend.at[t], wprecv.at[t], dev(c_=1 - c)).wait_recv()

    wp(0).start()
    wy(0, q0, 3, 1).start()
    wy(0, q0, 1, 2).start()
    wy(0, q0, 2, 3).start()
    wz().start()
    for d in (1, 2, 3):
        pl.semaphore_signal(tok_a, inc=1, device_id=dev(zl_=(zl + d) % 4), device_id_type=MESH)

    def split_s(d):
        scopy(d).wait()

        def body(n, _):
            rows = pl.ds(pl.multiple_of(((x + d) % 4) * BLK + n * 96, 96), 96)
            h, l = split(sv[rows, :])
            shi[rows, :] = h
            slo[rows, :] = l
            return 0

        lax.fori_loop(0, BLK // 96, body, 0)

    split_s(2)

    qc = zl * 2 + zh

    def c_out(d):
        return rc(ctp.at[c], ct.at[c, y * 2 + zh, x], csend.at[1 + d], crecv.at[1 + x], dev(y_=zl, zl_=y, x_=d))

    def c_keep():
        return pltpu.make_async_copy(ctp.at[c], ct.at[c, y * 2 + zh, x], lsem.at[6])

    def c_in(d):
        return rc(ctp.at[c], ct.at[c, qc, d], csend.at[1 + d], crecv.at[1 + d], dev(y_=zl, zl_=y, x_=d))

    diagonal = y == zl

    def unit(z_):
        return ((z_ % 4) * 2 + z_ // 4) % 8

    def ring_r(k):
        q = unit((z + 9 - k) % 8)
        return rc(ct.at[c, q], ct.at[c, q], rsend.at[0, k], rrecv.at[0, k], devz((z + 1) % 8))

    def ring_l(k):
        q = unit((z + k + 7) % 8)
        return rc(ct.at[c, q], ct.at[c, q], rsend.at[1, k], rrecv.at[1, k], devz((z + 7) % 8))

    def ring_r_in(k):
        q = unit((z + 8 - k) % 8)
        return rc(ct.at[c, q], ct.at[c, q], rsend.at[0, k], rrecv.at[0, k], devz((z + 7) % 8))

    def ring_l_in(k):
        q = unit((z + k) % 8)
        return rc(ct.at[c, q], ct.at[c, q], rsend.at[1, k], rrecv.at[1, k], devz((z + 1) % 8))

    def c_pair():
        return rc(ct.at[c], ct.at[c], psend.at[0], precv.at[0], dev(c_=1 - c))

    def c_pair_in():
        return rc(ct.at[1 - c], ct.at[1 - c], psend.at[0], precv.at[0], dev(c_=1 - c))

    def block(t, d):
        rows = pl.ds(pl.multiple_of(((x + d) % 4) * BLK, BLK), BLK)
        return three(nt, shi[rows, :], slo[rows, :], whi[t], wlo[t])

    def x_copy(t, m):
        src, dst, to = (
            (far.at[t, 0], fr.at[t, 0], xr),
            (far.at[t, 1], fr.at[t, 1], xl),
            (near.at[t, 0, 1], nr.at[t, 0, 1], xr),
            (near.at[t, 1, 0], nr.at[t, 1, 0], xl),
            (near.at[t, 0, 0], nr.at[t, 0, 0], xr),
            (near.at[t, 1, 1], nr.at[t, 1, 1], xl),
        )[m]
        return rc(src, dst, xsend.at[t, m], xrecv.at[t, m], dev(x_=to))

    def z_copy(t, d):
        return rc(zb.at[t, (zl + d) % 4], zr.at[t, d - 1], zsend.at[t, d - 1], zrecv.at[t, d - 1], dev(zl_=(zl + d) % 4))

    def y_copy(t, d):
        q = chunk(y, t)
        return rc(av.at[q, y], av.at[q, y], ysend.at[t, d - 1], yrecv.at[t, d - 1], dev(y_=(y + d) % 4))

    def y_in(t, d):
        yo = (y + 4 - d) % 4
        q = chunk(yo, t)
        return rc(av.at[q, yo], av.at[q, yo], ysend.at[t, d - 1], yrecv.at[t, d - 1], dev(y_=yo))

    def split_w(t):
        q = chunk(y, t)

        def body(n, _):
            h, l = split(wall[q, n])
            rows = pl.ds(pl.multiple_of(n * 64, 64), 64)
            whi[t, rows, :] = h
            wlo[t, rows, :] = l
            return 0

        lax.fori_loop(0, NC, body, 0)

    def far_step(t):
        far[t] = block(t, 2).reshape(2, HB, 128)
        x_copy(t, 0).start()
        x_copy(t, 1).start()

    def near_step(t):
        near[t, 0] = block(t, 1).reshape(2, HB, 128)
        x_copy(t, 2).start()
        near[t, 1] = block(t, 3).reshape(2, HB, 128)
        x_copy(t, 3).start()

    def join_step(t):
        for side in range(2):
            x_copy(t, side).wait_recv()
            near[t, side, side] = near[t, side, side] + fr[t, side]
            x_copy(t, 4 + side).start()

    def own_step(t):
        own[t] = block(t, 0).reshape(2, HB, 128)

    def x_finish(t):
        for m in range(2, 6):
            x_copy(t, m).wait_recv()
        for half in range(2):
            v = own[t, half] + nr[t, 0, half] + nr[t, 1, half]
            zb[t, 2 * half] = v[:SL]
            zb[t, 2 * half + 1] = v[SL:]
        for d in (2, 1, 3):
            z_copy(t, d).start()

    def keep(q, yo):
        h, l = split(av[q, yo])
        rows = pl.ds(pl.multiple_of(yo * 128, 128), SL)
        cols = pl.ds(pl.multiple_of(q * 128, 128), 128)
        ahi[rows, cols] = h
        alo[rows, cols] = l

    def z_finish(t):
        for d in (1, 2, 3):
            z_copy(t, d).wait_recv()
        q = chunk(y, t)
        av[q, y] = (zb[t, zl] + zr[t, 0]) + (zr[t, 1] + zr[t, 2])
        for d in (2, 1, 3):
            y_copy(t, d).start()
        keep(q, y)

    def y_finish(t):
        for d in (1, 2, 3):
            y_in(t, d).wait_recv()
            yo = (y + 4 - d) % 4
            keep(chunk(yo, t), yo)

    wp_arrived(0)
    split_w(0)
    far_step(0)
    for d in (1, 3):
        split_s(d)
    near_step(0)
    w_arrived(1)
    wp(1).start()
    split_s(0)

    ccopy.wait()
    ct_own = cv[...].T
    cz = jnp.zeros((64, 64), F32)
    at0 = jnp.concatenate([ct_own, cz], axis=1)
    at1 = jnp.concatenate([cz, ct_own], axis=1)
    ctp[...] = jnp.where(c == 0, at0, at1).reshape(2, 32, 128)

    def c_swap():
        return rc(ctp.at[1 - c], cx, csend.at[0], crecv.at[0], dev(c_=1 - c))

    c_swap().start()
    for slot in range(NY):
        ahi[128 * slot + SL : 128 * slot + 128, :] = jnp.zeros((128 - SL, 1024), BF16)
        alo[128 * slot + SL : 128 * slot + 128, :] = jnp.zeros((128 - SL, 1024), BF16)
    wp_arrived(1)
    split_w(1)
    far_step(1)
    w_arrived(2)
    wp(2).start()

    def step(t, _):
        join_step(t)

        @pl.when(t == 0)
        def _():
            w_arrived(3)
            wp(3).start()

        @pl.when(t == 1)
        def _():
            w_arrived(4)
            q = chunk(y, 4)
            wp(4).start()
            wy(4, q, 3, 5).start()
            wy(4, q, 1, 6).start()
            wy(4, q, 2, 7).start()

        @pl.when((t >= 2) & (t < 5))
        def _():
            w_arrived(t + 3)
            wp(t + 3).start()

        @pl.when(t < 7)
        def _():
            near_step(t + 1)

        @pl.when(t < 6)
        def _():
            wp_arrived(t + 2)
            split_w(t + 2)
            far_step(t + 2)

        @pl.when(t == 0)
        def _():
            pl.semaphore_wait(tok_a, 3)
            for d in (1, 2, 3):
                pl.semaphore_signal(tok_b, inc=1, device_id=dev(x_=(x + d) % 4), device_id_type=MESH)

        @pl.when(t == 1)
        def _():
            pl.semaphore_wait(tok_b, 3)
            c_swap().wait()
            ctp[c] = ctp[c] + cx[...]
            for d in range(4):

                @pl.when(jnp.logical_not(diagonal & (x == d)))
                def _(d=d):
                    c_out(d).start()

            @pl.when(diagonal)
            def _():
                c_keep().start()
                c_keep().wait()

        @pl.when(t == 2)
        def _():
            for d in range(4):

                @pl.when(jnp.logical_not(diagonal & (x == d)))
                def _(d=d):
                    c_in(d).wait_recv()
                    c_out(d).wait_send()

            ring_r(1).start()
            ring_l(1).start()

        @pl.when((t >= 3) & (t < 7))
        def _():
            ring_r_in(t - 2).wait_recv()
            ring_r(t - 2).wait_send()

        @pl.when((t >= 3) & (t < 6))
        def _():
            ring_r(t - 1).start()
            ring_l_in(t - 2).wait_recv()
            ring_l(t - 2).wait_send()

        @pl.when((t >= 3) & (t < 5))
        def _():
            ring_l(t - 1).start()

        @pl.when(t == 6)
        def _():
            c_pair().start()

        own_step(t)

        @pl.when(t >= 1)
        def _():
            x_finish(t - 1)

        @pl.when(t >= 2)
        def _():
            z_finish(t - 2)

        @pl.when(t >= 4)
        def _():
            y_finish(t - 4)

        return 0

    lax.fori_loop(0, CH, step, 0)
    c_pair().wait_send()
    c_pair_in().wait_recv()

    def split_c(q, _):
        cols = pl.ds(pl.multiple_of(q * 128, 128), 128)
        for half in range(2):
            h, l = split(ct[half, q].reshape(128, 128))
            chi[128 * half : 128 * half + 128, cols] = h
            clo[128 * half : 128 * half + 128, cols] = l
        return 0

    lax.fori_loop(0, 8, split_c, 0)

    def project(t, d):
        yo = (y + 4 - d) % 4
        cols = pl.ds(pl.multiple_of(chunk(yo, t) * 128, 128), 128)
        slot = pl.ds(pl.multiple_of(yo * 128, 128), 128)
        pt[:, slot] = pt[:, slot] + three(nt, chi[:, cols], clo[:, cols], ahi[slot, cols], alo[slot, cols])

    def project_some(n, _):
        project(n // 4, n % 4)
        return 0

    pt[...] = jnp.zeros_like(pt)
    lax.fori_loop(0, 4, project_some, 0)
    x_finish(7)
    z_finish(6)
    y_finish(4)
    lax.fori_loop(4, 20, project_some, 0)
    y_finish(5)
    lax.fori_loop(20, 24, project_some, 0)
    z_finish(7)
    y_finish(6)
    lax.fori_loop(24, 29, project_some, 0)
    y_finish(7)
    lax.fori_loop(29, 32, project_some, 0)

    h, l = split(pt[...] * pt[...])
    qhi[...] = h.reshape(2, 128, 512)
    qlo[...] = l.reshape(2, 128, 512)

    def moment_part(half, part):
        def body(n, _):
            cols = pl.ds(pl.multiple_of(part * 512 + n * 256, 256), 256)
            v = three(nn, qhi[half], qlo[half], ahi[:, cols], alo[:, cols])
            for u in range(2):
                mb[half, part, :, 2 * n + u] = v[:, 128 * u : 128 * u + 128].reshape(4, 32, 128)
            return 0

        lax.fori_loop(0, 2, body, 0)

    def m_pair(part):
        return rc(mb.at[1 - c, part], mp.at[part], psend.at[1 + part], precv.at[1 + part], dev(c_=1 - c))

    for part in range(2):
        moment_part(1 - c, part)
        m_pair(part).start()
    for part in range(2):
        moment_part(c, part)

    def m_copy(m):
        src, dst, to = (
            (ms.at[(x + 2) % 4, 0], mf.at[0], xr),
            (ms.at[(x + 2) % 4, 1], mf.at[1], xl),
            (ms.at[xr, 1], mr.at[0, 1], xr),
            (ms.at[xl, 0], mr.at[1, 0], xl),
            (ms.at[xr, 0], mr.at[0, 0], xr),
            (ms.at[xl, 1], mr.at[1, 1], xl),
        )[m]
        return rc(src, dst, msend.at[m], mrecv.at[m], dev(x_=to))

    def m_sum(b, part):
        ms[b, part] = mb[c, part, b] + mp[part, b]

    m_pair(0).wait_recv()
    m_sum((x + 2) % 4, 0)
    m_copy(0).start()
    m_sum(xl, 0)
    m_copy(3).start()
    m_pair(1).wait_recv()
    m_sum((x + 2) % 4, 1)
    m_copy(1).start()
    m_sum(xr, 1)
    m_copy(2).start()
    m_sum(xr, 0)
    m_copy(0).wait_recv()
    ms[xr, 0] = ms[xr, 0] + mf[0]
    m_copy(4).start()
    m_sum(xl, 1)
    m_copy(1).wait_recv()
    ms[xl, 1] = ms[xl, 1] + mf[1]
    m_copy(5).start()
    m_sum(x, 0)
    m_sum(x, 1)
    def f_out(q):
        return rc(fs.at[q], frec.at[z], fsend.at[q], frecv.at[z], dev(y_=q // 2, zh_=q % 2, zl_=y))

    def f_in(z_):
        return rc(fs.at[0], frec.at[z_], fsend.at[0], frecv.at[z_], devz(z_, y_=zl))

    mine = y * 2 + zh
    for part in range(2):
        m_copy(3 - part).wait_recv()
        m_copy(4 + part).wait_recv()
        fs[4 * part : 4 * part + 4] = ms[x, part] + (mr[0, part] + mr[1, part])
        for q in range(4 * part, 4 * part + 4):

            @pl.when(jnp.logical_not(diagonal & (q == mine)))
            def _(q=q):
                f_out(q).start()

    @pl.when(diagonal)
    def _():
        frec[z] = fs[mine]

    for z_ in range(8):

        @pl.when(jnp.logical_not(diagonal & (z == z_)))
        def _(z_=z_):
            f_in(z_).wait_recv()

    total = frec[0]
    for z_ in range(1, 8):
        total = total + frec[z_]
    gv[...] = total * (1.0 / 24576.0**0.5)
    swap = rc(gv, gr, psend.at[3], precv.at[3], dev(c_=1 - c))
    swap.start()
    ov[pl.ds(pl.multiple_of(c * 32, 32), 32), :] = gv[...]
    swap.wait_recv()
    ov[pl.ds(pl.multiple_of((1 - c) * 32, 32), 32), :] = gr[...]
    ot[...] = ov[...].T
    of[...] = ot[pl.ds(pl.multiple_of(c * 64, 64), 64), :]
    result = pltpu.make_async_copy(of, out_hbm, lsem.at[7])
    result.start()

    swap.wait_send()
    m_pair(0).wait_send()
    m_pair(1).wait_send()
    for m in range(6):
        m_copy(m).wait_send()
    for d in (1, 2, 3):
        wy(0, q0, d, d).wait_send()
        wy(4, chunk(y, 4), d, d).wait_send()
    wz().wait_send()
    for q in range(8):

        @pl.when(jnp.logical_not(diagonal & (q == mine)))
        def _(q=q):
            f_out(q).wait_send()

    def drain(t, _):
        wp(t).wait_send()
        for m in range(6):
            x_copy(t, m).wait_send()
        for d in (1, 2, 3):
            z_copy(t, d).wait_send()
            y_copy(t, d).wait_send()
        return 0

    lax.fori_loop(0, CH, drain, 0)
    result.wait()


def on_device(samples, whitening, components):
    V = pltpu.VMEM
    D = pltpu.SemaphoreType.DMA
    scratch = [
        V((ROWS_DEV, FD), F32), V((64, 64), F32),
        V((ROWS_DEV, FD), BF16), V((ROWS_DEV, FD), BF16),
        V((CH, NC, 64, FD), F32), V((CH, 128, FD), BF16), V((CH, 128, FD), BF16),
        V((CH, 2, HB, 128), F32), V((CH, 2, 2, HB, 128), F32), V((CH, 2, HB, 128), F32),
        V((CH, 2, HB, 128), F32), V((CH, 2, 2, HB, 128), F32),
        V((CH, 4, SL, 128), F32), V((CH, 3, SL, 128), F32),
        V((CH, NY, SL, 128), F32), V((512, 1024), BF16), V((512, 1024), BF16),
        V((2, 32, 128), F32), V((32, 128), F32), V((2, 8, 4, 32, 128), F32),
        V((256, 1024), BF16), V((256, 1024), BF16),
        V((256, 512), F32), V((2, 128, 512), BF16), V((2, 128, 512), BF16),
        V((2, 2, 4, 4, 32, 128), F32), V((2, 4, 4, 32, 128), F32), V((4, 2, 4, 32, 128), F32),
        V((2, 4, 32, 128), F32), V((2, 2, 4, 32, 128), F32), V((8, 32, 128), F32), V((8, 32, 128), F32),
        V((32, 128), F32), V((32, 128), F32), V((64, 128), F32), V((128, 64), F32), V((64, 64), F32),
        D((8,)), D((8,)), D((8,)), D((8,)), D((8,)),
        D((8, 6)), D((8, 6)), D((8, 3)), D((8, 3)), D((8, 3)), D((8, 3)),
        D((5,)), D((5,)), D((2, 5)), D((2, 5)), D((4,)), D((4,)), D((6,)), D((6,)), D((8,)), D((8,)),
        pltpu.SemaphoreType.REGULAR, pltpu.SemaphoreType.REGULAR,
    ]
    return pl.pallas_call(
        kernel,
        out_shape=jax.ShapeDtypeStruct((64, 64), F32),
        in_specs=[pl.BlockSpec(memory_space=pl.ANY)] * 3,
        out_specs=pl.BlockSpec(memory_space=pl.ANY),
        scratch_shapes=scratch,
        compiler_params=pltpu.CompilerParams(
            collective_id=0, has_side_effects=True, vmem_limit_bytes=60 * 1024 * 1024
        ),
    )(samples, whitening.T, components)


def solution(mesh):
    placed = (P("rows", "feat"), P("feat", "rows"), P("rows", "feat"))
    return jax.shard_map(
        on_device, mesh=mesh, in_specs=placed, out_specs=P("rows", "feat"), check_vma=False
    )
```

```python
import jax
import jax.numpy as jnp
from jax import lax
from jax.experimental import pallas as pl
from jax.experimental.pallas import tpu as pltpu
from jax.sharding import PartitionSpec as P

MESH = pl.DeviceIdType.MESH
F32 = jnp.float32
BF16 = jnp.bfloat16
NX, NY, NZH, NZL, NC = 4, 4, 2, 4, 2
NZ = NZH * NZL
CH = NY * NZH
ROWS_DEV = 1536
BLK = ROWS_DEV // NX
HB = BLK // 2
SL = BLK // NZL
FD = 512


def split(v):
    hi = v.astype(BF16)
    return hi, (v - hi.astype(F32)).astype(BF16)


def nt(a, b):
    return lax.dot_general(a, b, (((1,), (1,)), ((), ())), preferred_element_type=F32)


def nn(a, b):
    return lax.dot_general(a, b, (((1,), (0,)), ((), ())), preferred_element_type=F32)


def three(dot, ah, al, bh, bl):
    return dot(ah, bh) + (dot(ah, bl) + dot(al, bh))


def kernel(
    s_hbm, w_hbm, c_hbm, out_hbm,
    sv, cv, shi, slo, wall, whi, wlo,
    far, near, own, fr, nr, zb, zr, av, ahi, alo,
    ctp, cx, ct, chi, clo, pt, qhi, qlo, mb, mp, ms, mf, mr, fs, frec, gv, gr, ov, ot, of,
    lsem, wsend, wrecv, wpsend, wprecv, xsend, xrecv, zsend, zrecv, ysend, yrecv,
    csend, crecv, rsend, rrecv, psend, precv, msend, mrecv, fsend, frecv, tok_a, tok_b,
):
    i, j = lax.axis_index("rows"), lax.axis_index("feat")
    y, zh, c = i // 4, (i // 2) % 2, i % 2
    zl, x = j // 4, j % 4
    z = zh * 4 + zl
    xl, xr = (x + 3) % 4, (x + 1) % 4

    def dev(y_=None, zh_=None, c_=None, zl_=None, x_=None):
        y_ = y if y_ is None else y_
        zh_ = zh if zh_ is None else zh_
        c_ = c if c_ is None else c_
        zl_ = zl if zl_ is None else zl_
        x_ = x if x_ is None else x_
        return (y_ * 4 + zh_ * 2 + c_, zl_ * 4 + x_)

    def devz(z_, **kw):
        return dev(zh_=z_ // 4, zl_=z_ % 4, **kw)

    def rc(src, dst, ss, rs, to):
        return pltpu.make_async_remote_copy(
            src_ref=src, dst_ref=dst, send_sem=ss, recv_sem=rs, device_id=to, device_id_type=MESH
        )

    def chunk(y_, t):
        u = t % 4
        dy = u + (u // 2) * (1 - 2 * (u % 2))
        return ((y_ + dy) % 4) * 2 + (zh + t // 4) % 2

    def lane(q):
        return (q % 2) * 4 + q // 2

    q0 = chunk(y, 0)
    wcopy = pltpu.make_async_copy(w_hbm, wall.at[q0, c], lsem.at[0])
    ccopy = pltpu.make_async_copy(c_hbm, cv, lsem.at[1])
    wcopy.start()

    def scopy(d):
        rows = pl.ds(pl.multiple_of(((x + d) % 4) * BLK, BLK), BLK)
        return pltpu.make_async_copy(s_hbm.at[rows], sv.at[rows], lsem.at[2 + d])

    for d in (2, 1, 3, 0):
        scopy(d).start()
    ccopy.start()

    barrier = pltpu.get_barrier_semaphore()
    partners = [dev(x_=(x + d) % 4) for d in (1, 2, 3)]
    partners += [dev(y_=(y + d) % 4) for d in (1, 2, 3)]
    partners += [dev(zl_=(zl + d) % 4) for d in (1, 2, 3)]
    partners += [dev(zh_=1 - zh), dev(c_=1 - c), devz((z + 1) % 8), devz((z + 7) % 8)]
    for p in partners:
        pl.semaphore_signal(barrier, inc=1, device_id=p, device_id_type=MESH)

    wcopy.wait()
    pl.semaphore_wait(barrier, len(partners))

    def wy(base, q, d, t):
        return rc(wall.at[q, c], wall.at[q, c], wsend.at[base + d], wrecv.at[t], dev(y_=(y + d) % 4))

    def wz():
        return rc(wall.at[q0, c], wall.at[q0, c], wsend.at[4], wrecv.at[4], dev(zh_=1 - zh))

    def wp(t):
        q = chunk(y, t)
        return rc(wall.at[q, c], wall.at[q, c], wpsend.at[t], wprecv.at[t], dev(c_=1 - c))

    def w_arrived(t):
        q = chunk(y, t)
        rc(wall.at[q, c], wall.at[q, c], wsend.at[0], wrecv.at[t], dev(c_=1 - c)).wait_recv()

    def wp_arrived(t):
        q = chunk(y, t)
        rc(wall.at[q, c], wall.at[q, 1 - c], wpsend.at[t], wprecv.at[t], dev(c_=1 - c)).wait_recv()

    wp(0).start()
    wy(0, q0, 3, 1).start()
    wy(0, q0, 1, 2).start()
    wy(0, q0, 2, 3).start()
    wz().start()
    for d in (1, 2, 3):
        pl.semaphore_signal(tok_a, inc=1, device_id=dev(zl_=(zl + d) % 4), device_id_type=MESH)

    def split_s(d):
        scopy(d).wait()

        def body(n, _):
            rows = pl.ds(pl.multiple_of(((x + d) % 4) * BLK + n * 96, 96), 96)
            h, l = split(sv[rows, :])
            shi[rows, :] = h
            slo[rows, :] = l
            return 0

        lax.fori_loop(0, BLK // 96, body, 0)

    split_s(2)

    qc = zl * 2 + zh

    def c_out(d):
        return rc(ctp.at[c], ct.at[c, y * 2 + zh, x], csend.at[1 + d], crecv.at[1 + x], dev(y_=zl, zl_=y, x_=d))

    def c_keep():
        return pltpu.make_async_copy(ctp.at[c], ct.at[c, y * 2 + zh, x], lsem.at[6])

    def c_in(d):
        return rc(ctp.at[c], ct.at[c, qc, d], csend.at[1 + d], crecv.at[1 + d], dev(y_=zl, zl_=y, x_=d))

    diagonal = y == zl

    def unit(z_):
        return ((z_ % 4) * 2 + z_ // 4) % 8

    def ring_r(k):
        q = unit((z + 9 - k) % 8)
        return rc(ct.at[c, q], ct.at[c, q], rsend.at[0, k], rrecv.at[0, k], devz((z + 1) % 8))

    def ring_l(k):
        q = unit((z + k + 7) % 8)
        return rc(ct.at[c, q], ct.at[c, q], rsend.at[1, k], rrecv.at[1, k], devz((z + 7) % 8))

    def ring_r_in(k):
        q = unit((z + 8 - k) % 8)
        return rc(ct.at[c, q], ct.at[c, q], rsend.at[0, k], rrecv.at[0, k], devz((z + 7) % 8))

    def ring_l_in(k):
        q = unit((z + k) % 8)
        return rc(ct.at[c, q], ct.at[c, q], rsend.at[1, k], rrecv.at[1, k], devz((z + 1) % 8))

    def c_pair():
        return rc(ct.at[c], ct.at[c], psend.at[0], precv.at[0], dev(c_=1 - c))

    def c_pair_in():
        return rc(ct.at[1 - c], ct.at[1 - c], psend.at[0], precv.at[0], dev(c_=1 - c))

    def block(t, d):
        rows = pl.ds(pl.multiple_of(((x + d) % 4) * BLK, BLK), BLK)
        return three(nt, shi[rows, :], slo[rows, :], whi[t], wlo[t])

    def x_copy(t, m):
        src, dst, to = (
            (far.at[t, 0], fr.at[t, 0], xr),
            (far.at[t, 1], fr.at[t, 1], xl),
            (near.at[t, 0, 1], nr.at[t, 0, 1], xr),
            (near.at[t, 1, 0], nr.at[t, 1, 0], xl),
            (near.at[t, 0, 0], nr.at[t, 0, 0], xr),
            (near.at[t, 1, 1], nr.at[t, 1, 1], xl),
        )[m]
        return rc(src, dst, xsend.at[t, m], xrecv.at[t, m], dev(x_=to))

    def z_copy(t, d):
        return rc(zb.at[t, (zl + d) % 4], zr.at[t, d - 1], zsend.at[t, d - 1], zrecv.at[t, d - 1], dev(zl_=(zl + d) % 4))

    def y_copy(t, d):
        q = chunk(y, t)
        return rc(av.at[q, y], av.at[q, y], ysend.at[t, d - 1], yrecv.at[t, d - 1], dev(y_=(y + d) % 4))

    def y_in(t, d):
        yo = (y + 4 - d) % 4
        q = chunk(yo, t)
        return rc(av.at[q, yo], av.at[q, yo], ysend.at[t, d - 1], yrecv.at[t, d - 1], dev(y_=yo))

    def split_w(t):
        q = chunk(y, t)

        def body(n, _):
            h, l = split(wall[q, n])
            rows = pl.ds(pl.multiple_of(n * 64, 64), 64)
            whi[t, rows, :] = h
            wlo[t, rows, :] = l
            return 0

        lax.fori_loop(0, NC, body, 0)

    def far_step(t):
        far[t] = block(t, 2).reshape(2, HB, 128)
        x_copy(t, 0).start()
        x_copy(t, 1).start()

    def near_step(t):
        near[t, 0] = block(t, 1).reshape(2, HB, 128)
        x_copy(t, 2).start()
        near[t, 1] = block(t, 3).reshape(2, HB, 128)
        x_copy(t, 3).start()

    def join_step(t):
        for side in range(2):
            x_copy(t, side).wait_recv()
            near[t, side, side] = near[t, side, side] + fr[t, side]
            x_copy(t, 4 + side).start()

    def own_step(t):
        own[t] = block(t, 0).reshape(2, HB, 128)

    def x_finish(t):
        for m in range(2, 6):
            x_copy(t, m).wait_recv()
        for half in range(2):
            v = own[t, half] + nr[t, 0, half] + nr[t, 1, half]
            zb[t, 2 * half] = v[:SL]
            zb[t, 2 * half + 1] = v[SL:]
        for d in (2, 1, 3):
            z_copy(t, d).start()

    def keep(q, yo):
        h, l = split(av[q, yo])
        rows = pl.ds(pl.multiple_of(yo * 128, 128), SL)
        cols = pl.ds(pl.multiple_of(lane(q) * 128, 128), 128)
        ahi[rows, cols] = h
        alo[rows, cols] = l

    def z_finish(t):
        for d in (1, 2, 3):
            z_copy(t, d).wait_recv()
        q = chunk(y, t)
        av[q, y] = (zb[t, zl] + zr[t, 0]) + (zr[t, 1] + zr[t, 2])
        for d in (2, 1, 3):
            y_copy(t, d).start()
        keep(q, y)

    def y_finish(t):
        for d in (1, 2, 3):
            y_in(t, d).wait_recv()
            yo = (y + 4 - d) % 4
            keep(chunk(yo, t), yo)

    wp_arrived(0)
    split_w(0)
    far_step(0)
    for d in (1, 3):
        split_s(d)
    near_step(0)
    w_arrived(1)
    wp(1).start()
    split_s(0)

    ccopy.wait()
    ct_own = cv[...].T
    cz = jnp.zeros((64, 64), F32)
    at0 = jnp.concatenate([ct_own, cz], axis=1)
    at1 = jnp.concatenate([cz, ct_own], axis=1)
    ctp[...] = jnp.where(c == 0, at0, at1).reshape(2, 32, 128)

    def c_swap():
        return rc(ctp.at[1 - c], cx, csend.at[0], crecv.at[0], dev(c_=1 - c))

    c_swap().start()
    for slot in range(NY):
        ahi[128 * slot + SL : 128 * slot + 128, :] = jnp.zeros((128 - SL, 1024), BF16)
        alo[128 * slot + SL : 128 * slot + 128, :] = jnp.zeros((128 - SL, 1024), BF16)
    wp_arrived(1)
    split_w(1)
    far_step(1)
    w_arrived(2)
    wp(2).start()

    def step(t, _):
        join_step(t)

        @pl.when(t == 0)
        def _():
            w_arrived(3)
            wp(3).start()

        @pl.when(t == 1)
        def _():
            w_arrived(4)
            q = chunk(y, 4)
            wp(4).start()
            wy(4, q, 3, 5).start()
            wy(4, q, 1, 6).start()
            wy(4, q, 2, 7).start()

        @pl.when((t >= 2) & (t < 5))
        def _():
            w_arrived(t + 3)
            wp(t + 3).start()

        @pl.when(t < 7)
        def _():
            near_step(t + 1)

        @pl.when(t < 6)
        def _():
            wp_arrived(t + 2)
            split_w(t + 2)
            far_step(t + 2)

        @pl.when(t == 0)
        def _():
            pl.semaphore_wait(tok_a, 3)
            for d in (1, 2, 3):
                pl.semaphore_signal(tok_b, inc=1, device_id=dev(x_=(x + d) % 4), device_id_type=MESH)

        @pl.when(t == 1)
        def _():
            pl.semaphore_wait(tok_b, 3)
            c_swap().wait()
            ctp[c] = ctp[c] + cx[...]
            for d in range(4):

                @pl.when(jnp.logical_not(diagonal & (x == d)))
                def _(d=d):
                    c_out(d).start()

            @pl.when(diagonal)
            def _():
                c_keep().start()
                c_keep().wait()

        @pl.when(t == 2)
        def _():
            for d in range(4):

                @pl.when(jnp.logical_not(diagonal & (x == d)))
                def _(d=d):
                    c_in(d).wait_recv()
                    c_out(d).wait_send()

            ring_r(1).start()
            ring_l(1).start()

        @pl.when((t >= 3) & (t < 7))
        def _():
            ring_r_in(t - 2).wait_recv()
            ring_r(t - 2).wait_send()

        @pl.when((t >= 3) & (t < 6))
        def _():
            ring_r(t - 1).start()
            ring_l_in(t - 2).wait_recv()
            ring_l(t - 2).wait_send()

        @pl.when((t >= 3) & (t < 5))
        def _():
            ring_l(t - 1).start()

        @pl.when(t == 6)
        def _():
            c_pair().start()

        own_step(t)

        @pl.when(t >= 1)
        def _():
            x_finish(t - 1)

        @pl.when(t >= 2)
        def _():
            z_finish(t - 2)

        @pl.when(t >= 4)
        def _():
            y_finish(t - 4)

        return 0

    lax.fori_loop(0, CH, step, 0)
    c_pair().wait_send()
    c_pair_in().wait_recv()

    def split_c(q, _):
        cols = pl.ds(pl.multiple_of(lane(q) * 128, 128), 128)
        for half in range(2):
            h, l = split(ct[half, q].reshape(128, 128))
            chi[128 * half : 128 * half + 128, cols] = h
            clo[128 * half : 128 * half + 128, cols] = l
        return 0

    lax.fori_loop(0, 8, split_c, 0)

    def project(t, d):
        yo = (y + 4 - d) % 4
        cols = pl.ds(pl.multiple_of(lane(chunk(yo, t)) * 128, 128), 128)
        slot = pl.ds(pl.multiple_of(yo * 128, 128), 128)
        pt[:, slot] = pt[:, slot] + three(nt, chi[:, cols], clo[:, cols], ahi[slot, cols], alo[slot, cols])

    def project_some(n, _):
        project(n // 4, n % 4)
        return 0

    x_finish(7)
    z_finish(6)
    y_finish(4)

    def project_side(n, _):
        rows = pl.ds(pl.multiple_of(n * 128, 128), 128)
        cols = pl.ds(pl.multiple_of(zh * 512, 512), 512)
        pt[rows, :] = three(nt, chi[rows, cols], clo[rows, cols], ahi[:, cols], alo[:, cols])
        return 0

    lax.fori_loop(0, 2, project_side, 0)
    lax.fori_loop(16, 20, project_some, 0)
    y_finish(5)
    lax.fori_loop(20, 24, project_some, 0)
    z_finish(7)
    y_finish(6)
    lax.fori_loop(24, 29, project_some, 0)
    y_finish(7)
    lax.fori_loop(29, 32, project_some, 0)

    h, l = split(pt[...] * pt[...])
    qhi[...] = h.reshape(2, 128, 512)
    qlo[...] = l.reshape(2, 128, 512)

    def moment_part(half, part):
        def body(n, _):
            cols = pl.ds(pl.multiple_of(part * 512 + n * 256, 256), 256)
            v = three(nn, qhi[half], qlo[half], ahi[:, cols], alo[:, cols])
            for u in range(2):
                mb[half, part, :, 2 * n + u] = v[:, 128 * u : 128 * u + 128].reshape(4, 32, 128)
            return 0

        lax.fori_loop(0, 2, body, 0)

    def m_pair(part):
        return rc(mb.at[1 - c, part], mp.at[part], psend.at[1 + part], precv.at[1 + part], dev(c_=1 - c))

    for part in range(2):
        moment_part(1 - c, part)
        m_pair(part).start()
    for part in range(2):
        moment_part(c, part)

    def m_copy(m):
        src, dst, to = (
            (ms.at[(x + 2) % 4, 0], mf.at[0], xr),
            (ms.at[(x + 2) % 4, 1], mf.at[1], xl),
            (ms.at[xr, 1], mr.at[0, 1], xr),
            (ms.at[xl, 0], mr.at[1, 0], xl),
            (ms.at[xr, 0], mr.at[0, 0], xr),
            (ms.at[xl, 1], mr.at[1, 1], xl),
        )[m]
        return rc(src, dst, msend.at[m], mrecv.at[m], dev(x_=to))

    def m_sum(b, part):
        ms[b, part] = mb[c, part, b] + mp[part, b]

    m_pair(0).wait_recv()
    m_sum((x + 2) % 4, 0)
    m_copy(0).start()
    m_sum(xl, 0)
    m_copy(3).start()
    m_pair(1).wait_recv()
    m_sum((x + 2) % 4, 1)
    m_copy(1).start()
    m_sum(xr, 1)
    m_copy(2).start()
    m_sum(xr, 0)
    m_copy(0).wait_recv()
    ms[xr, 0] = ms[xr, 0] + mf[0]
    m_copy(4).start()
    m_sum(xl, 1)
    m_copy(1).wait_recv()
    ms[xl, 1] = ms[xl, 1] + mf[1]
    m_copy(5).start()
    m_sum(x, 0)
    m_sum(x, 1)
    def f_out(q):
        return rc(fs.at[q], frec.at[z], fsend.at[q], frecv.at[z], dev(y_=q % 4, zh_=q // 4, zl_=y))

    def f_in(z_):
        return rc(fs.at[0], frec.at[z_], fsend.at[0], frecv.at[z_], devz(z_, y_=zl))

    mine = zh * 4 + y
    for part in range(2):
        m_copy(3 - part).wait_recv()
        m_copy(4 + part).wait_recv()
        fs[4 * part : 4 * part + 4] = ms[x, part] + (mr[0, part] + mr[1, part])
        for q in range(4 * part, 4 * part + 4):

            @pl.when(jnp.logical_not(diagonal & (q == mine)))
            def _(q=q):
                f_out(q).start()

    @pl.when(diagonal)
    def _():
        frec[z] = fs[mine]

    for z_ in range(8):

        @pl.when(jnp.logical_not(diagonal & (z == z_)))
        def _(z_=z_):
            f_in(z_).wait_recv()

    total = frec[0]
    for z_ in range(1, 8):
        total = total + frec[z_]
    gv[...] = total * (1.0 / 24576.0**0.5)
    swap = rc(gv, gr, psend.at[3], precv.at[3], dev(c_=1 - c))
    swap.start()
    ov[pl.ds(pl.multiple_of(c * 32, 32), 32), :] = gv[...]
    swap.wait_recv()
    ov[pl.ds(pl.multiple_of((1 - c) * 32, 32), 32), :] = gr[...]
    ot[...] = ov[...].T
    of[...] = ot[pl.ds(pl.multiple_of(c * 64, 64), 64), :]
    result = pltpu.make_async_copy(of, out_hbm, lsem.at[7])
    result.start()

    swap.wait_send()
    m_pair(0).wait_send()
    m_pair(1).wait_send()
    for m in range(6):
        m_copy(m).wait_send()
    for d in (1, 2, 3):
        wy(0, q0, d, d).wait_send()
        wy(4, chunk(y, 4), d, d).wait_send()
    wz().wait_send()
    for q in range(8):

        @pl.when(jnp.logical_not(diagonal & (q == mine)))
        def _(q=q):
            f_out(q).wait_send()

    def drain(t, _):
        wp(t).wait_send()
        for m in range(6):
            x_copy(t, m).wait_send()
        for d in (1, 2, 3):
            z_copy(t, d).wait_send()
            y_copy(t, d).wait_send()
        return 0

    lax.fori_loop(0, CH, drain, 0)
    result.wait()


def on_device(samples, whitening, components):
    V = pltpu.VMEM
    D = pltpu.SemaphoreType.DMA
    scratch = [
        V((ROWS_DEV, FD), F32), V((64, 64), F32),
        V((ROWS_DEV, FD), BF16), V((ROWS_DEV, FD), BF16),
        V((CH, NC, 64, FD), F32), V((CH, 128, FD), BF16), V((CH, 128, FD), BF16),
        V((CH, 2, HB, 128), F32), V((CH, 2, 2, HB, 128), F32), V((CH, 2, HB, 128), F32),
        V((CH, 2, HB, 128), F32), V((CH, 2, 2, HB, 128), F32),
        V((CH, 4, SL, 128), F32), V((CH, 3, SL, 128), F32),
        V((CH, NY, SL, 128), F32), V((512, 1024), BF16), V((512, 1024), BF16),
        V((2, 32, 128), F32), V((32, 128), F32), V((2, 8, 4, 32, 128), F32),
        V((256, 1024), BF16), V((256, 1024), BF16),
        V((256, 512), F32), V((2, 128, 512), BF16), V((2, 128, 512), BF16),
        V((2, 2, 4, 4, 32, 128), F32), V((2, 4, 4, 32, 128), F32), V((4, 2, 4, 32, 128), F32),
        V((2, 4, 32, 128), F32), V((2, 2, 4, 32, 128), F32), V((8, 32, 128), F32), V((8, 32, 128), F32),
        V((32, 128), F32), V((32, 128), F32), V((64, 128), F32), V((128, 64), F32), V((64, 64), F32),
        D((8,)), D((8,)), D((8,)), D((8,)), D((8,)),
        D((8, 6)), D((8, 6)), D((8, 3)), D((8, 3)), D((8, 3)), D((8, 3)),
        D((5,)), D((5,)), D((2, 5)), D((2, 5)), D((4,)), D((4,)), D((6,)), D((6,)), D((8,)), D((8,)),
        pltpu.SemaphoreType.REGULAR, pltpu.SemaphoreType.REGULAR,
    ]
    return pl.pallas_call(
        kernel,
        out_shape=jax.ShapeDtypeStruct((64, 64), F32),
        in_specs=[pl.BlockSpec(memory_space=pl.ANY)] * 3,
        out_specs=pl.BlockSpec(memory_space=pl.ANY),
        scratch_shapes=scratch,
        compiler_params=pltpu.CompilerParams(
            collective_id=0, has_side_effects=True, vmem_limit_bytes=60 * 1024 * 1024
        ),
    )(samples, whitening.T, components)


def solution(mesh):
    placed = (P("rows", "feat"), P("feat", "rows"), P("rows", "feat"))
    return jax.shard_map(
        on_device, mesh=mesh, in_specs=placed, out_specs=P("rows", "feat"), check_vma=False
    )
```
